32 devices in a mesh: groups: 2 (over y), lanes: 4 (over z), heads: 2 (over x), rep: 2 (over core).
Axes of the slice: x: 2, y: 2, z: 4, core: 2. Of those that a mesh axis runs over, the one named last changes fastest.
Arguments:
- queries: bfloat16 [4096, 2048], P(('groups', 'lanes'), ('heads', 'rep')), parts along dimension 0, may hold values from -6 to 6
- span_states: bfloat16 [4096, 896], P(('groups', 'lanes')), parts along dimension 0, may hold values from -6 to 6
- store: bfloat16 [128, 128, 896], P(('groups', 'lanes'), ('heads', 'rep')), parts along dimension 0, may hold values from -480 to 480
- entry_ids: int32 [64, 2], P(('groups', 'lanes')), parts along dimension 0, may hold values from 0 to 15
- owners: int32 [64, 2], P(('groups', 'lanes')), parts along dimension 0, may hold values from 0 to 3, as said below
- w_key: bfloat16 [896, 2048], P(None, ('heads', 'rep')), may hold values from -0.1875 to 0.1875
- w_value: bfloat16 [896, 2048], P(None, ('heads', 'rep')), may hold values from -0.1875 to 0.1875
- w_out: bfloat16 [2048, 4096], P(('heads', 'rep')), may hold values from -0.125 to 0.125
Outputs:
- attended: bfloat16 [4096, 4096], P(('groups', 'lanes', 'heads', 'rep')), parts along dimension 0
The draws below stay inside these ranges and needn't reach their ends.
There are 2 independent parts, one for each index of `groups`. The reference program is written for one: setup_inputs(seed, part) draws one part's arguments, and reference() takes and returns one part's arrays. A program takes and returns all parts, laid end to end along the dimension named above; an argument that names none is the same for every part. Nothing has to cross between parts.
Inputs may be any that keep to these rules, and one draw needn't show every extreme that they name: Among the 16 neighbours of one lane's spans at most 4 have the same owner, the 2 owners of a span differ, and in every draw one owner holds 4 neighbours of every lane.
All inputs are finite; a program needn't handle non-finite values.
Results may differ from the reference program's by a relative error of at most 0.014.
The reference program's roundings to bfloat16 on the way count: a program that leaves them out, or rounds other values in their place, can miss the bound.
Values may be sent and summed in bfloat16 or wider, within the bound.
A program may use at most 128 MiB of HBM per device.

```python
import jax
import jax.numpy as jnp
from jax import lax

D = 4096
H = 16
HD = 128
E = 896
ENCODER_HEAD_DIM = 128
CL = 64
K = 2
NT = 128
CHD = 8
ENT_DEV = 16
SPANS = 32
TOKENS = 2048
ENTRIES = 64
CAP = 4
N_LANES = 4
N_HEADS = 2
N_REP = 2


def lane_permutation(lane_key):
    return jax.random.permutation(lane_key, N_LANES - 1)


def span_reordering(lane_key):
    return jax.random.permutation(lane_key, CHD)


def draw_owners(key, part):
    base = jax.random.fold_in(key, 7)
    hot_key, perm_key, row_key = jax.random.split(base, 3)
    hottest = jax.random.randint(hot_key, (), 0, N_LANES).astype(jnp.int32)
    others = jax.vmap(lane_permutation)(jax.random.split(perm_key, N_LANES)).astype(jnp.int32)
    others = others + (others >= hottest).astype(jnp.int32)
    position = jnp.arange(K * CHD, dtype=jnp.int32)
    group_index = jnp.maximum(position - CAP, 0) // CAP
    picked = jnp.take(others, group_index, axis=1)
    layout_plan = jnp.where(position[None, :] < CAP, hottest, picked).reshape(N_LANES, K, CHD)
    shuffle = jax.vmap(span_reordering)(jax.random.split(row_key, N_LANES)).astype(jnp.int32)
    shuffled = jnp.take_along_axis(layout_plan, shuffle[:, None, :], axis=2)
    return jnp.transpose(shuffled, (0, 2, 1)).reshape(SPANS, K).astype(jnp.int32)


def draw_store(key, part):
    base = jax.random.fold_in(key, 3)
    value_key = jax.random.fold_in(base, 0)
    values = jnp.clip(jax.random.normal(value_key, (ENTRIES, NT, E), jnp.float32), -6.0, 6.0)
    return values.astype(jnp.bfloat16)


def plant(drawn, stream_key, least, top_value):
    longest = drawn.shape.index(max(drawn.shape))
    spots = []
    for shift in (0, 1):
        where = [jax.random.randint(jax.random.fold_in(stream_key, axis), (), 0, length) for axis, length in enumerate(drawn.shape)]
        where[longest] = (where[longest] + shift) % drawn.shape[longest]
        spots.append(tuple(where))
    return drawn.at[spots[0]].set(least).at[spots[1]].set(top_value)


def block_scale(rng, extent, shards, smallest, high):
    def one(dim, blocks):
        steps = jax.random.uniform(jax.random.fold_in(jax.random.fold_in(rng, 6), dim), (blocks,), jnp.float32, smallest / len(shards), high / len(shards))
        return jnp.repeat(jnp.exp(steps), extent[dim] // blocks).reshape((-1,) + (1,) * (len(extent) - dim - 1))

    level = one(*shards[0])
    for cut in shards[1:]:
        level = level * one(*cut)
    return level


def gaussian(key, shape, scale, bound, cuts=(), kind=jnp.bfloat16):
    values = jax.random.normal(key, shape, jnp.float32) * scale
    if len(cuts) > 0:
        values = block_scale(key, shape, cuts, -0.22, 0.18) * values
    return jnp.clip(values, min=-bound, max=bound).astype(kind)


def setup_inputs(seed: int = 0, part: int = 0) -> dict:
    seeds = jax.random.split(jax.random.key(seed), 9)
    part_keys = jax.random.split(jax.random.fold_in(seeds[8], part), 9)
    return {
        "queries": gaussian(part_keys[0], (TOKENS, H * HD), 1.0, 6.0, ((0, 4), (1, 4))),
        "span_states": gaussian(part_keys[1], (TOKENS, E), 1.0, 6.0, ((0, 4),)),
        "store": draw_store(jax.random.fold_in(jax.random.fold_in(seeds[8], part), 71), part),
        "entry_ids": plant(jax.random.randint(part_keys[3], (SPANS, K), 0, ENT_DEV), jax.random.fold_in(part_keys[3], 1), 0, ENT_DEV - 1).astype(jnp.int32),
        "owners": draw_owners(jax.random.fold_in(jax.random.fold_in(seeds[8], part), 71), part),
        "w_key": gaussian(seeds[5], (E, H * HD), E ** -0.5, 0.1875, ((1, 4),)),
        "w_value": gaussian(seeds[6], (E, H * HD), E ** -0.5, 0.1875, ((1, 4),)),
        "w_out": gaussian(seeds[7], (H * HD, D), (H * HD) ** -0.5, 0.125, ((0, 4),)),
    }


def reference(queries, span_states, store, entry_ids, owners, w_key, w_value, w_out):
    global_rows = (owners * ENT_DEV + entry_ids).astype(jnp.int32)
    enc_heads = E // ENCODER_HEAD_DIM

    def one_span(span_item):
        query_rows, state_rows, chosen = span_item
        tokens = jnp.take(store, chosen, axis=0).reshape(K * NT, E).astype(jnp.float32)
        states = state_rows.astype(jnp.float32)
        token_head_rows = tokens.reshape(K * NT, enc_heads, ENCODER_HEAD_DIM)
        head_states = states.reshape(CL, enc_heads, ENCODER_HEAD_DIM)
        score_logits = jnp.einsum("qil,bil->iqb", token_head_rows, head_states) * (ENCODER_HEAD_DIM ** -0.5)
        attention_result = lax.optimization_barrier(jax.nn.softmax(score_logits, axis=-1).astype(jnp.bfloat16))
        attention_result = attention_result.astype(jnp.float32)
        mixed_input = jnp.einsum("cni,icx->ncx", attention_result, head_states)
        encoded = (tokens + mixed_input.reshape(K * NT, E)).astype(jnp.bfloat16)
        key_rows = jnp.dot(encoded, w_key, preferred_element_type=jnp.float32).astype(jnp.bfloat16)
        value_rows = jnp.dot(encoded, w_value, preferred_element_type=jnp.float32).astype(jnp.bfloat16)
        query_heads = query_rows.astype(jnp.float32).reshape(CL, H, HD)
        key_heads = key_rows.astype(jnp.float32).reshape(K * NT, H, HD)
        value_heads = value_rows.astype(jnp.float32).reshape(K * NT, H, HD)
        scores = jnp.einsum("qhd,khd->hqk", query_heads, key_heads) * (HD ** -0.5)
        softmax_rows = lax.optimization_barrier(jax.nn.softmax(scores, axis=-1).astype(jnp.bfloat16))
        softmax_rows = softmax_rows.astype(jnp.float32)
        result = jnp.einsum("hqk,khd->qhd", softmax_rows, value_heads)
        return result.reshape(CL, H * HD).astype(jnp.bfloat16)

    heads_out = lax.map(one_span, (queries.reshape(SPANS, CL, H * HD), span_states.reshape(SPANS, CL, E), global_rows))
    heads_out = heads_out.reshape(TOKENS, H * HD)
    groups = N_HEADS * N_REP
    group_width = (H * HD) // groups
    pieces = jnp.transpose(heads_out.reshape(TOKENS, groups, group_width), (1, 0, 2))
    weights = w_out.reshape(groups, group_width, D)

    def add_group(running, operands):
        partial_value = jnp.dot(operands[0], operands[1], preferred_element_type=jnp.float32).astype(jnp.bfloat16)
        partial_value = lax.optimization_barrier(partial_value)
        return running + partial_value.astype(jnp.float32), None

    running, unused = lax.scan(add_group, jnp.zeros((TOKENS, D), jnp.float32), (pieces, weights))
    return running.astype(jnp.bfloat16)
```

```python
import functools
import itertools

import jax
import jax.numpy as jnp
from jax import lax
from jax.experimental import pallas as pl
from jax.experimental.pallas import tpu as pltpu
from jax.sharding import PartitionSpec as P

HD = 128
ENCODER_HEAD_DIM = 128
MESH = pl.DeviceIdType.MESH
F32 = jnp.float32
BF16 = jnp.bfloat16


def softmax_parts(parts):
    top = functools.reduce(jnp.maximum, [jnp.max(p, axis=-1, keepdims=True) for p in parts])
    exps = [jnp.exp(p - top) for p in parts]
    total = functools.reduce(jnp.add, [jnp.sum(e, axis=-1, keepdims=True) for e in exps])
    inv = 1.0 / total
    return [(e * inv).astype(BF16) for e in exps]


def dot_t(a, b):
    return lax.dot_general(a, b, (((1,), (1,)), ((), ())), preferred_element_type=F32)


def early_spans(n_x, n_lanes, cap, spans, fanout):
    whole = n_x == 2 and cap == n_lanes == 4 and fanout == 2 and spans == 2 * n_lanes
    return spans // n_x // 2 if whole else 0


def fused(
    n_lanes, n_x, n_c, cap, n_cols,
    owner_ref, entry_ref, query_hbm, states_hbm, store_hbm, wk_hbm, wv_hbm, wo_hbm,
    out_ref,
    query_v, states_v, store_v, wk_v, wv_v, wo_v,
    table, span_table, span_sm, own_sm, got_sm, rank_sm, virtual_sm, slot_sm,
    send_tok, recv_tok, enc, keys, values, heads_out,
    part, part_in, summed, summed_in, final, final_out,
    load_sem, local_sem, idx_send, idx_recv, tok_sends, tok_recvs, x_send, c_send, x_recvs, c_recvs,
    part_send, part_recv, sum_send, sum_recv, final_send, final_recv,
):
    lane = lax.axis_index("lanes")
    x = lax.axis_index("heads")
    c = lax.axis_index("rep")
    mate = n_c - 1 - c
    fanout, spans = owner_ref.shape
    requests = spans * fanout
    width = store_v.shape[2]
    span_len = query_v.shape[1]
    chip_spans = spans // n_x
    core_spans = chip_spans // n_c
    col = wo_v.shape[1] // n_cols
    half = span_len // n_c
    quarter = x * n_c + c
    early = early_spans(n_x, n_lanes, cap, spans, fanout)
    stages = part.shape[1]
    batch = chip_spans // stages

    loads = [
        pltpu.make_async_copy(src, dst, load_sem.at[i])
        for i, (src, dst) in enumerate(
            (
                (store_hbm, store_v),
                (states_hbm, states_v),
                (wk_hbm, wk_v),
                (wv_hbm, wv_v),
                (query_hbm, query_v),
                (wo_hbm, wo_v),
            )
        )
    ]
    for load in loads[:2]:
        load.start()

    barrier = pltpu.get_barrier_semaphore()
    for d in range(1, n_lanes):
        pl.semaphore_signal(barrier, inc=1, device_id={"lanes": lax.rem(lane + d, n_lanes)}, device_id_type=MESH)
    for d in range(1, n_x):
        pl.semaphore_signal(barrier, inc=1, device_id={"heads": lax.rem(x + d, n_x)}, device_id_type=MESH)
    pl.semaphore_signal(barrier, inc=1, device_id={"rep": mate}, device_id_type=MESH)

    owner = [owner_ref[j % fanout, j // fanout] for j in range(requests)]
    ranks = []
    if early:
        word = [
            sum(jnp.where(owner[s * fanout + f] == o, 1 << (4 * o), 0) for f in range(fanout) for o in range(n_lanes))
            for s in range(spans)
        ]
        target = sum((cap // 2) << (4 * o) for o in range(n_lanes))
        chosen = list(itertools.combinations(range(chip_spans), early))
        sums = [[sum(word[h * chip_spans + s] for s in some) for some in chosen] for h in range(n_x)]
        mask = jnp.int32(0)
        for a, some in enumerate(chosen):
            for b, others in enumerate(chosen):
                bits = sum(1 << s for s in some) + sum(1 << (chip_spans + s) for s in others)
                mask = jnp.where(sums[0][a] + sums[1][b] == target, bits, mask)
        first, later = jnp.int32(0), jnp.int32(target)
        slot = []
        for s in range(spans):
            if s % chip_spans == 0:
                n_first, n_later = jnp.int32(0), jnp.int32(early)
            taken = ((mask >> s) & 1) == 1
            ahead = jnp.where(taken, first, later)
            for f in range(fanout):
                ranks.append(
                    sum(jnp.where(owner[s * fanout + f] == o, (ahead >> (4 * o)) & 15, 0) for o in range(n_lanes))
                )
            first, later = first + jnp.where(taken, word[s], 0), later + jnp.where(taken, 0, word[s])
            slot.append(jnp.where(taken, n_first, n_later))
            n_first, n_later = n_first + jnp.where(taken, 1, 0), n_later + jnp.where(taken, 0, 1)
        for s in range(spans):
            base = s // chip_spans * chip_spans
            slot_sm[s] = jnp.minimum(slot[s], chip_spans - 1)
            virtual_sm[s] = sum(jnp.where(slot[base + i] == s - base, base + i, 0) for i in range(chip_spans))
    else:
        for j in range(requests):
            ranks.append(sum((owner[i] == owner[j]).astype(jnp.int32) for i in range(j)) + jnp.int32(0))
        for s in range(spans):
            slot_sm[s] = s % chip_spans
            virtual_sm[s] = s
    place = lax.broadcasted_iota(jnp.int32, table.shape, 1)
    entries = jnp.zeros(table.shape, jnp.int32)
    whose = jnp.zeros(table.shape, jnp.int32)
    for j, rank in enumerate(ranks):
        rank_sm[j] = jnp.minimum(rank, cap - 1)
        hit = place == owner[j] * cap + rank
        entries = jnp.where(hit, entry_ref[j % fanout, j // fanout], entries)
        whose = jnp.where(hit, j // fanout, whose)
    table[...] = entries
    span_table[...] = whose
    pl.semaphore_wait(barrier, n_lanes + n_x - 1)

    def idx_copy(d):
        return pltpu.make_async_remote_copy(
            src_ref=table, dst_ref=got_sm.at[lane], send_sem=idx_send.at[d], recv_sem=idx_recv.at[d],
            device_id={"lanes": lax.rem(lane + d, n_lanes)}, device_id_type=MESH,
        )

    for d in range(1, n_lanes):
        idx_copy(d).start()
    to_sm = pltpu.make_async_copy(span_table, span_sm, local_sem.at[0])
    to_sm.start()
    own_to_sm = pltpu.make_async_copy(table, own_sm, local_sem.at[1])
    own_to_sm.start()
    to_sm.wait()
    own_to_sm.wait()
    loads[0].wait()
    loads[1].wait()
    for load in loads[2:]:
        load.start()

    def tok_copy(r, d):
        return pltpu.make_async_remote_copy(
            src_ref=send_tok.at[r, d], dst_ref=recv_tok.at[r, d],
            send_sem=tok_sends.at[r], recv_sem=tok_recvs.at[r, d],
            device_id={"lanes": lax.rem(lane + d, n_lanes)}, device_id_type=MESH,
        )

    def sent(ref, sem):
        pltpu.make_async_remote_copy(
            src_ref=ref, dst_ref=ref, send_sem=sem, recv_sem=sem, device_id={"rep": mate}, device_id_type=MESH
        ).wait_send()

    def toks_sent(r):
        sent(send_tok.at[r, pl.ds(1, n_lanes - 1)], tok_sends.at[r])

    def send_one(r, d):
        who = lax.rem(lane + d, n_lanes)
        send_tok[r, d] = store_v[got_sm[who, 0, lane * cap + r]]
        tok_copy(r, d).start()

    def send_rank(r):
        def one(d, carry):
            send_one(r, d)
            return carry

        lax.fori_loop(1, n_lanes, one, 0)

    def x_copy(r, s, d):
        return pltpu.make_async_remote_copy(
            src_ref=enc.at[r, s, quarter], dst_ref=enc.at[r, s, quarter],
            send_sem=x_send.at[0], recv_sem=x_recvs.at[r, s, d - 1],
            device_id={"heads": lax.rem(x + d, n_x)}, device_id_type=MESH,
        )

    def c_copy(r, s, block):
        return pltpu.make_async_remote_copy(
            src_ref=enc.at[r, s, block], dst_ref=enc.at[r, s, block],
            send_sem=c_send.at[0], recv_sem=c_recvs.at[r],
            device_id={"rep": mate}, device_id_type=MESH,
        )

    def source(d):
        return lax.rem(lane - d + n_lanes, n_lanes)

    def encode(group, fetch):
        tokens = [fetch(r, d) for r, d in group]
        states = [states_v[span_sm[0, source(d) * cap + r]] for r, d in group]
        heads = [
            (n, slice(h * ENCODER_HEAD_DIM, (h + 1) * ENCODER_HEAD_DIM))
            for n in range(len(group))
            for h in range(width // ENCODER_HEAD_DIM)
        ]
        logits = [dot_t(tokens[n][:, cols], states[n][:, cols]) * ENCODER_HEAD_DIM ** (-0.5) for n, cols in heads]
        weights = [softmax_parts([logit])[0] for logit in logits]
        mixed = [
            jnp.dot(weight, states[n][:, cols], preferred_element_type=F32) for weight, (n, cols) in zip(weights, heads)
        ]
        for mix, (n, cols) in zip(mixed, heads):
            r, d = group[n]
            enc[r, source(d), quarter, :, cols] = (tokens[n][:, cols].astype(F32) + mix).astype(BF16)
        for r, d in group:
            s = source(d)
            for k in range(1, n_x):
                x_copy(r, s, k).start()
            c_copy(r, s, quarter).start()

    def relay(r, d):
        s = source(d)
        for k in range(1, n_x):
            block = lax.rem(x - k + n_x, n_x) * n_c + c
            pltpu.make_async_remote_copy(
                src_ref=enc.at[r, s, block], dst_ref=enc.at[r, s, block],
                send_sem=x_send.at[0], recv_sem=x_recvs.at[r, s, k - 1],
                device_id={"rep": mate}, device_id_type=MESH,
            ).wait_recv()
            c_copy(r, s, block).start()

    encode([(r, 0) for r in range(cap)], lambda r, d: store_v[own_sm[0, lane * cap + r]])
    ahead = min(2, cap)
    for d in sorted(range(1, n_lanes), key=lambda d: min(d, n_lanes - d)):
        idx_copy(d).wait_recv()
        send_one(0, n_lanes - d)
    for r in range(1, ahead):
        send_rank(r)
    groups = n_lanes - 1
    total = cap * groups
    lag = min(2, groups)
    lane_chunk = min(n_lanes, 4)

    def settle(r):
        ref = enc.at[r, :, pl.ds(0, n_x)]
        pltpu.make_async_remote_copy(
            src_ref=ref, dst_ref=ref, send_sem=c_send.at[0], recv_sem=c_recvs.at[r],
            device_id={"rep": mate}, device_id_type=MESH,
        ).wait_recv()

    def project(r):
        settle(r)

        def chunk(g, carry):
            some = pl.ds(g * lane_chunk, lane_chunk)
            rows = enc[r, some].reshape(-1, width)
            for weight, target in ((wk_v, keys), (wv_v, values)):
                result = jnp.dot(rows, weight[...], preferred_element_type=F32).astype(BF16)
                target[r, some] = result.reshape((lane_chunk,) + target.shape[2:])
            return carry

        lax.fori_loop(0, n_lanes // lane_chunk, chunk, 0)

    def attend(k, e):
        first = lax.rem(x + k + 1, n_x) * chip_spans + e * batch
        which = [virtual_sm[first + n] for n in range(batch)]
        slots = [[(rank_sm[s * fanout + f], owner_ref[f, s]) for f in range(fanout)] for s in which]
        heads = [(n, slice(h * HD, (h + 1) * HD)) for n in range(batch) for h in range(query_v.shape[2] // HD)]
        logits = [
            [dot_t(query_v[which[n], :, cols], keys[r, o, :, cols]) * HD ** (-0.5) for r, o in slots[n]]
            for n, cols in heads
        ]
        weights = [softmax_parts(parts) for parts in logits]
        mixed = [
            functools.reduce(
                jnp.add,
                [
                    jnp.dot(w, values[r, o, :, cols], preferred_element_type=F32)
                    for w, (r, o) in zip(parts, slots[n])
                ],
            )
            for parts, (n, cols) in zip(weights, heads)
        ]
        for mix, (n, cols) in zip(mixed, heads):
            heads_out[n, :, cols] = mix.astype(BF16)

    def part_copy(k, e, j):
        return pltpu.make_async_remote_copy(
            src_ref=part.at[k, e, j, mate], dst_ref=part_in.at[k, e, j],
            send_sem=part_send.at[0], recv_sem=part_recv.at[k, e, j],
            device_id={"rep": mate}, device_id_type=MESH,
        )

    def sum_copy(k, e, j):
        return pltpu.make_async_remote_copy(
            src_ref=summed.at[k, e, j], dst_ref=summed_in.at[k, e, j],
            send_sem=sum_send.at[0], recv_sem=sum_recv.at[k, e, j],
            device_id={"heads": lax.rem(x + k + 1, n_x)}, device_id_type=MESH,
        )

    def columns(j):
        return pl.ds(pl.multiple_of(j * col, col), col)

    def product(k, e, j):
        rows = heads_out[...].reshape(-1, heads_out.shape[2])
        result = jnp.dot(rows, wo_v[:, columns(j)], preferred_element_type=F32).astype(BF16)
        result = result.reshape((batch, n_c, half, col))
        for core in range(n_c):
            for n in range(batch):
                part[k, e, j, core, n] = result[n, core]
        part_copy(k, e, j).start()

    def combine(k, e, j):
        part_copy(k, e, j).wait_recv()
        both = part[k, e, j, c].astype(F32) + part_in[k, e, j].astype(F32)
        summed[k, e, j] = both.astype(BF16)
        sum_copy(k, e, j).start()

    def products(k, e):
        attend(k, e)

        def step(j, carry):
            product(k, e, j)
            return carry

        lax.fori_loop(0, n_cols, step, 0)

    def combines(k, e, lo, hi):
        def step(j, carry):
            combine(k, e, j)
            return carry

        lax.fori_loop(lo, hi, step, 0)

    own = n_x - 1
    ready = cap // 2 - 1

    def slot_step(i, carry):
        r, d = i // groups, 1 + i % groups
        tok_copy(r, d).wait_recv()
        encode([(r, d)], lambda r, d: recv_tok[r, d])

        @pl.when(i == lag - 1)
        def _():
            for n in range(cap):
                relay(n, 0)

        @pl.when(i >= lag)
        def _():
            relay((i - lag) // groups, 1 + (i - lag) % groups)

        for n in range(ahead, cap):

            @pl.when(i == (n - 1) * groups - 1)
            def _():
                toks_sent(n - ahead)
                send_rank(n)

        @pl.when(i == groups + lag - 1)
        def _():
            loads[2].wait()
            loads[3].wait()

        for n in range(cap - 1):

            @pl.when(i == (n + 1) * groups + lag - 1)
            def _():
                project(n)
                if early and n == ready:
                    loads[4].wait()
                    loads[5].wait()
                    for k in range(own):
                        products(k, 0)
                if early and n == ready + 1:
                    for k in range(own):
                        combines(k, 0, 1, 2)

        if early:

            @pl.when(i == (ready + 2) * groups)
            def _():
                for k in range(own):
                    combines(k, 0, 0, 1)

        return carry

    lax.fori_loop(0, total, slot_step, 0)
    if early:
        for k in range(own):
            combines(k, 0, 2, n_cols // 2)
        products(own, 0)
        for k in range(own):
            combines(k, 0, n_cols // 2, n_cols)
    else:
        loads[4].wait()
        loads[5].wait()

    def late_relay(i, carry):
        relay(i // groups, 1 + i % groups)
        return carry

    lax.fori_loop(total - lag, total, late_relay, 0)
    project(cap - 1)
    last = stages - 1
    behind = min(5, n_cols)
    for k in range(own):
        attend(k, last)

        def late(j, carry):
            @pl.when(j < n_cols)
            def _():
                product(k, last, j)

            @pl.when(j >= behind)
            def _():
                combine(k, last, j - behind)

            return carry

        lax.fori_loop(0, n_cols + behind, late, 0)
    products(own, last)

    def final_copy(j, n):
        rows = pl.ds(pl.multiple_of(n * span_len + c * half, half), half)
        return pltpu.make_async_remote_copy(
            src_ref=final_out.at[j, n], dst_ref=out_ref.at[rows, columns(j)],
            send_sem=final_send.at[0], recv_sem=final_recv.at[0],
            device_id={"rep": mate}, device_id_type=MESH,
        )

    def finish(j, carry):
        for e in range(stages):
            part_copy(own, e, j).wait_recv()
            total = part[own, e, j, c].astype(F32) + part_in[own, e, j].astype(F32)
            for k in range(own):
                sum_copy(k, e, j).wait_recv()
                total = total + summed_in[k, e, j].astype(F32)
            final[e * batch : (e + 1) * batch] = total.astype(BF16)
        for n in range(core_spans):
            first = x * chip_spans + n
            final_out[j, n] = final[slot_sm[first + mate * core_spans]]
            final_copy(j, n).start()
            rows = pl.ds(pl.multiple_of(n * span_len + c * half, half), half)
            out_ref[rows, columns(j)] = final[slot_sm[first + c * core_spans]]
        return carry

    lax.fori_loop(0, n_cols, finish, 0)
    for d in range(1, n_lanes):
        idx_copy(d).wait_send()
    for r in range(cap - ahead, cap):
        toks_sent(r)
    sent(enc.at[:, :, pl.ds(0, n_x - 1)], x_send.at[0])
    sent(enc.at[:, :, pl.ds(0, n_x)], c_send.at[0])
    sent(part_in, part_send.at[0])
    sent(summed, sum_send.at[0])
    sent(final_out, final_send.at[0])
    pltpu.make_async_remote_copy(
        src_ref=final_out, dst_ref=final_out, send_sem=final_send.at[0], recv_sem=final_recv.at[0],
        device_id={"rep": mate}, device_id_type=MESH,
    ).wait_recv()


def shards(queries, span_states, store, entry_ids, owners, w_key, w_value, w_out):
    n_lanes, n_x, n_c = (lax.axis_size(name) for name in ("lanes", "heads", "rep"))
    spans, fanout = entry_ids.shape
    requests = spans * fanout
    cap = max(2, (requests + n_lanes - 1) // n_lanes)
    span_len = queries.shape[0] // spans
    tok_dev, width = store.shape[1:]
    tokens = tok_dev * n_x * n_c
    head_cols, model = w_out.shape
    out_rows = queries.shape[0] // (n_x * n_c)
    n_cols = 8
    core_spans = spans // (n_x * n_c)
    chip_spans = spans // n_x
    stages = 2 if early_spans(n_x, n_lanes, cap, spans, fanout) else 1
    batch = chip_spans // stages
    half = span_len // n_c
    col = model // n_cols
    lanes_wide = -(-(n_lanes * cap) // 128) * 128
    dma = pltpu.SemaphoreType.DMA
    hbm = pl.BlockSpec(memory_space=pl.ANY)
    smem = pl.BlockSpec(memory_space=pltpu.SMEM)
    return pl.pallas_call(
        functools.partial(fused, n_lanes, n_x, n_c, cap, n_cols),
        out_shape=pltpu.VMEM((out_rows, model), BF16),
        in_specs=[smem, smem] + [hbm] * 6,
        out_specs=pl.BlockSpec(memory_space=pltpu.VMEM),
        scratch_shapes=[
            pltpu.VMEM((spans, span_len, head_cols), BF16),
            pltpu.VMEM((spans, span_len, width), BF16),
            pltpu.VMEM(store.shape, BF16),
            pltpu.VMEM(w_key.shape, BF16),
            pltpu.VMEM(w_value.shape, BF16),
            pltpu.VMEM(w_out.shape, BF16),
            pltpu.VMEM((8, lanes_wide), jnp.int32),
            pltpu.VMEM((8, lanes_wide), jnp.int32),
            pltpu.SMEM((8, lanes_wide), jnp.int32),
            pltpu.SMEM((8, lanes_wide), jnp.int32),
            pltpu.SMEM((n_lanes, 8, lanes_wide), jnp.int32),
            pltpu.SMEM((requests,), jnp.int32),
            pltpu.SMEM((spans,), jnp.int32),
            pltpu.SMEM((spans,), jnp.int32),
            pltpu.VMEM((cap, n_lanes, tok_dev, width), BF16),
            pltpu.VMEM((cap, n_lanes, tok_dev, width), BF16),
            pltpu.VMEM((cap, n_lanes, n_x * n_c, tok_dev, width), BF16),
            pltpu.VMEM((cap, n_lanes, tokens, head_cols), BF16),
            pltpu.VMEM((cap, n_lanes, tokens, head_cols), BF16),
            pltpu.VMEM((batch, span_len, head_cols), BF16),
            pltpu.VMEM((n_x, stages, n_cols, n_c, batch, half, col), BF16),
            pltpu.VMEM((n_x, stages, n_cols, batch, half, col), BF16),
            pltpu.VMEM((n_x - 1, stages, n_cols, batch, half, col), BF16),
            pltpu.VMEM((n_x - 1, stages, n_cols, batch, half, col), BF16),
            pltpu.VMEM((chip_spans, half, col), BF16),
            pltpu.VMEM((n_cols, core_spans, half, col), BF16),
            dma((6,)),
            dma((2,)),
            dma((n_lanes,)),
            dma((n_lanes,)),
            dma((cap,)),
            dma((cap, n_lanes)),
            dma((1,)),
            dma((1,)),
            dma((cap, n_lanes, n_x - 1)),
            dma((cap,)),
            dma((1,)),
            dma((n_x, stages, n_cols)),
            dma((1,)),
            dma((n_x - 1, stages, n_cols)),
            dma((1,)),
            dma((1,)),
        ],
        compiler_params=pltpu.CompilerParams(
            collective_id=0, has_side_effects=True, vmem_limit_bytes=60000000
        ),
    )(
        owners.T,
        entry_ids.T,
        queries.reshape(spans, span_len, head_cols),
        span_states.reshape(spans, span_len, width),
        store,
        w_key,
        w_value,
        w_out,
    )


def solution(mesh):
    return jax.shard_map(
        shards,
        mesh=mesh,
        in_specs=(
            P(("groups", "lanes"), ("heads", "rep")),
            P(("groups", "lanes"), None),
            P(("groups", "lanes"), ("heads", "rep"), None),
            P(("groups", "lanes"), None),
            P(("groups", "lanes"), None),
            P(None, ("heads", "rep")),
            P(None, ("heads", "rep")),
            P(("heads", "rep"), None),
        ),
        out_specs=P(("groups", "lanes", "heads", "rep"), None),
        check_vma=False,
    )
```

```python
import functools
import itertools

import jax
import jax.numpy as jnp
from jax import lax
from jax.experimental import pallas as pl
from jax.experimental.pallas import tpu as pltpu
from jax.sharding import PartitionSpec as P

HD = 128
ENCODER_HEAD_DIM = 128
MESH = pl.DeviceIdType.MESH
F32 = jnp.float32
BF16 = jnp.bfloat16


def softmax_parts(parts):
    top = functools.reduce(jnp.maximum, [jnp.max(p, axis=-1, keepdims=True) for p in parts])
    exps = [jnp.exp(p - top) for p in parts]
    total = functools.reduce(jnp.add, [jnp.sum(e, axis=-1, keepdims=True) for e in exps])
    inv = 1.0 / total
    return [(e * inv).astype(BF16) for e in exps]


def dot_t(a, b):
    return lax.dot_general(a, b, (((1,), (1,)), ((), ())), preferred_element_type=F32)


def early_spans(n_x, n_lanes, cap, spans, fanout):
    whole = n_x == 2 and cap == n_lanes == 4 and fanout == 2 and spans == 2 * n_lanes
    return spans // n_x // 2 if whole else 0


def fused(
    n_lanes, n_x, n_c, cap, n_cols,
    owner_ref, entry_ref, query_hbm, states_hbm, store_hbm, wk_hbm, wv_hbm, wo_hbm,
    out_ref,
    query_v, states_v, store_v, wk_v, wv_v, wo_v,
    table, span_table, span_sm, own_sm, got_sm, rank_sm, virtual_sm, slot_sm,
    send_tok, recv_tok, enc, keys, values, heads_out,
    part, part_in, summed, summed_in, final, final_out,
    load_sem, local_sem, idx_send, idx_recv, tok_sends, tok_recvs, x_send, c_send, x_recvs, c_recvs,
    part_send, part_recv, sum_send, sum_recv, final_send, final_recv,
):
    lane = lax.axis_index("lanes")
    x = lax.axis_index("heads")
    c = lax.axis_index("rep")
    mate = n_c - 1 - c
    fanout, spans = owner_ref.shape
    requests = spans * fanout
    width = store_v.shape[2]
    span_len = query_v.shape[1]
    chip_spans = spans // n_x
    core_spans = chip_spans // n_c
    col = wo_v.shape[1] // n_cols
    half = span_len // n_c
    quarter = x * n_c + c
    early = early_spans(n_x, n_lanes, cap, spans, fanout)
    stages = part.shape[1]
    batch = chip_spans // stages

    loads = [
        pltpu.make_async_copy(src, dst, load_sem.at[i])
        for i, (src, dst) in enumerate(
            (
                (store_hbm, store_v),
                (states_hbm, states_v),
                (wk_hbm, wk_v),
                (wv_hbm, wv_v),
                (query_hbm, query_v),
                (wo_hbm, wo_v),
            )
        )
    ]
    for load in loads[:2]:
        load.start()

    barrier = pltpu.get_barrier_semaphore()
    for d in range(1, n_lanes):
        pl.semaphore_signal(barrier, inc=1, device_id={"lanes": lax.rem(lane + d, n_lanes)}, device_id_type=MESH)
    for d in range(1, n_x):
        pl.semaphore_signal(barrier, inc=1, device_id={"heads": lax.rem(x + d, n_x)}, device_id_type=MESH)
    pl.semaphore_signal(barrier, inc=1, device_id={"rep": mate}, device_id_type=MESH)

    owner = [owner_ref[j % fanout, j // fanout] for j in range(requests)]
    ranks = []
    if early:
        word = [
            sum(jnp.where(owner[s * fanout + f] == o, 1 << (4 * o), 0) for f in range(fanout) for o in range(n_lanes))
            for s in range(spans)
        ]
        target = sum((cap // 2) << (4 * o) for o in range(n_lanes))
        chosen = list(itertools.combinations(range(chip_spans), early))
        sums = [[sum(word[h * chip_spans + s] for s in some) for some in chosen] for h in range(n_x)]
        mask = jnp.int32(0)
        for a, some in enumerate(chosen):
            for b, others in enumerate(chosen):
                bits = sum(1 << s for s in some) + sum(1 << (chip_spans + s) for s in others)
                mask = jnp.where(sums[0][a] + sums[1][b] == target, bits, mask)
        first, later = jnp.int32(0), jnp.int32(target)
        slot = []
        for s in range(spans):
            if s % chip_spans == 0:
                n_first, n_later = jnp.int32(0), jnp.int32(early)
            taken = ((mask >> s) & 1) == 1
            ahead = jnp.where(taken, first, later)
            for f in range(fanout):
                ranks.append(
                    sum(jnp.where(owner[s * fanout + f] == o, (ahead >> (4 * o)) & 15, 0) for o in range(n_lanes))
                )
            first, later = first + jnp.where(taken, word[s], 0), later + jnp.where(taken, 0, word[s])
            slot.append(jnp.where(taken, n_first, n_later))
            n_first, n_later = n_first + jnp.where(taken, 1, 0), n_later + jnp.where(taken, 0, 1)
        for s in range(spans):
            base = s // chip_spans * chip_spans
            slot_sm[s] = jnp.minimum(slot[s], chip_spans - 1)
            virtual_sm[s] = sum(jnp.where(slot[base + i] == s - base, base + i, 0) for i in range(chip_spans))
    else:
        for j in range(requests):
            ranks.append(sum((owner[i] == owner[j]).astype(jnp.int32) for i in range(j)) + jnp.int32(0))
        for s in range(spans):
            slot_sm[s] = s % chip_spans
            virtual_sm[s] = s
    place = lax.broadcasted_iota(jnp.int32, table.shape, 1)
    entries = jnp.zeros(table.shape, jnp.int32)
    whose = jnp.zeros(table.shape, jnp.int32)
    for j, rank in enumerate(ranks):
        rank_sm[j] = jnp.minimum(rank, cap - 1)
        hit = place == owner[j] * cap + rank
        entries = jnp.where(hit, entry_ref[j % fanout, j // fanout], entries)
        whose = jnp.where(hit, j // fanout, whose)
    table[...] = entries
    span_table[...] = whose
    pl.semaphore_wait(barrier, n_lanes + n_x - 1)

    def idx_copy(d):
        return pltpu.make_async_remote_copy(
            src_ref=table, dst_ref=got_sm.at[lane], send_sem=idx_send.at[d], recv_sem=idx_recv.at[d],
            device_id={"lanes": lax.rem(lane + d, n_lanes)}, device_id_type=MESH,
        )

    for d in range(1, n_lanes):
        idx_copy(d).start()
    to_sm = pltpu.make_async_copy(span_table, span_sm, local_sem.at[0])
    to_sm.start()
    own_to_sm = pltpu.make_async_copy(table, own_sm, local_sem.at[1])
    own_to_sm.start()
    to_sm.wait()
    own_to_sm.wait()
    loads[0].wait()
    loads[1].wait()
    for load in loads[2:]:
        load.start()

    def tok_copy(r, d):
        return pltpu.make_async_remote_copy(
            src_ref=send_tok.at[r, d], dst_ref=recv_tok.at[r, d],
            send_sem=tok_sends.at[r], recv_sem=tok_recvs.at[r, d],
            device_id={"lanes": lax.rem(lane + d, n_lanes)}, device_id_type=MESH,
        )

    def sent(ref, sem):
        pltpu.make_async_remote_copy(
            src_ref=ref, dst_ref=ref, send_sem=sem, recv_sem=sem, device_id={"rep": mate}, device_id_type=MESH
        ).wait_send()

    def toks_sent(r):
        sent(send_tok.at[r, pl.ds(1, n_lanes - 1)], tok_sends.at[r])

    def send_one(r, d):
        who = lax.rem(lane + d, n_lanes)
        send_tok[r, d] = store_v[got_sm[who, 0, lane * cap + r]]
        tok_copy(r, d).start()

    def send_rank(r):
        def one(d, carry):
            send_one(r, d)
            return carry

        lax.fori_loop(1, n_lanes, one, 0)

    def x_copy(r, s, d):
        return pltpu.make_async_remote_copy(
            src_ref=enc.at[r, s, quarter], dst_ref=enc.at[r, s, quarter],
            send_sem=x_send.at[0], recv_sem=x_recvs.at[r, s, d - 1],
            device_id={"heads": lax.rem(x + d, n_x)}, device_id_type=MESH,
        )

    def c_copy(r, s, block):
        return pltpu.make_async_remote_copy(
            src_ref=enc.at[r, s, block], dst_ref=enc.at[r, s, block],
            send_sem=c_send.at[0], recv_sem=c_recvs.at[r],
            device_id={"rep": mate}, device_id_type=MESH,
        )

    def source(d):
        return lax.rem(lane - d + n_lanes, n_lanes)

    def encode(group, fetch):
        tokens = [fetch(r, d) for r, d in group]
        states = [states_v[span_sm[0, source(d) * cap + r]] for r, d in group]
        heads = [
            (n, slice(h * ENCODER_HEAD_DIM, (h + 1) * ENCODER_HEAD_DIM))
            for n in range(len(group))
            for h in range(width // ENCODER_HEAD_DIM)
        ]
        logits = [dot_t(tokens[n][:, cols], states[n][:, cols]) * ENCODER_HEAD_DIM ** (-0.5) for n, cols in heads]
        weights = [softmax_parts([logit])[0] for logit in logits]
        mixed = [
            jnp.dot(weight, states[n][:, cols], preferred_element_type=F32) for weight, (n, cols) in zip(weights, heads)
        ]
        for mix, (n, cols) in zip(mixed, heads):
            r, d = group[n]
            enc[r, source(d), quarter, :, cols] = (tokens[n][:, cols].astype(F32) + mix).astype(BF16)
        for r, d in group:
            s = source(d)
            for k in range(1, n_x):
                x_copy(r, s, k).start()
            c_copy(r, s, quarter).start()

    def relay(r, d):
        s = source(d)
        for k in range(1, n_x):
            block = lax.rem(x - k + n_x, n_x) * n_c + c
            pltpu.make_async_remote_copy(
                src_ref=enc.at[r, s, block], dst_ref=enc.at[r, s, block],
                send_sem=x_send.at[0], recv_sem=x_recvs.at[r, s, k - 1],
                device_id={"rep": mate}, device_id_type=MESH,
            ).wait_recv()
            c_copy(r, s, block).start()

    encode([(r, 0) for r in range(cap)], lambda r, d: store_v[own_sm[0, lane * cap + r]])
    ahead = min(2, cap)
    for d in sorted(range(1, n_lanes), key=lambda d: min(d, n_lanes - d)):
        idx_copy(d).wait_recv()
        send_one(0, n_lanes - d)
    for r in range(1, ahead):
        send_rank(r)
    groups = n_lanes - 1
    total = cap * groups
    lag = min(3, groups)
    lane_chunk = min(n_lanes, 4)

    def settle(r):
        ref = enc.at[r, :, pl.ds(0, n_x)]
        pltpu.make_async_remote_copy(
            src_ref=ref, dst_ref=ref, send_sem=c_send.at[0], recv_sem=c_recvs.at[r],
            device_id={"rep": mate}, device_id_type=MESH,
        ).wait_recv()

    def project(r):
        settle(r)

        def chunk(g, carry):
            some = pl.ds(g * lane_chunk, lane_chunk)
            rows = enc[r, some].reshape(-1, width)
            for weight, target in ((wk_v, keys), (wv_v, values)):
                result = jnp.dot(rows, weight[...], preferred_element_type=F32).astype(BF16)
                target[r, some] = result.reshape((lane_chunk,) + target.shape[2:])
            return carry

        lax.fori_loop(0, n_lanes // lane_chunk, chunk, 0)

    def attend(k, e):
        first = lax.rem(x + k + 1, n_x) * chip_spans + e * batch
        which = [virtual_sm[first + n] for n in range(batch)]
        slots = [[(rank_sm[s * fanout + f], owner_ref[f, s]) for f in range(fanout)] for s in which]
        heads = [(n, slice(h * HD, (h + 1) * HD)) for n in range(batch) for h in range(query_v.shape[2] // HD)]
        logits = [
            [dot_t(query_v[which[n], :, cols], keys[r, o, :, cols]) * HD ** (-0.5) for r, o in slots[n]]
            for n, cols in heads
        ]
        weights = [softmax_parts(parts) for parts in logits]
        mixed = [
            functools.reduce(
                jnp.add,
                [
                    jnp.dot(w, values[r, o, :, cols], preferred_element_type=F32)
                    for w, (r, o) in zip(parts, slots[n])
                ],
            )
            for parts, (n, cols) in zip(weights, heads)
        ]
        for mix, (n, cols) in zip(mixed, heads):
            heads_out[n, :, cols] = mix.astype(BF16)

    def part_copy(k, e, j):
        return pltpu.make_async_remote_copy(
            src_ref=part.at[k, e, j, mate], dst_ref=part_in.at[k, e, j],
            send_sem=part_send.at[0], recv_sem=part_recv.at[k, e, j],
            device_id={"rep": mate}, device_id_type=MESH,
        )

    def sum_copy(k, e, j):
        return pltpu.make_async_remote_copy(
            src_ref=summed.at[k, e, j], dst_ref=summed_in.at[k, e, j],
            send_sem=sum_send.at[0], recv_sem=sum_recv.at[k, e, j],
            device_id={"heads": lax.rem(x + k + 1, n_x)}, device_id_type=MESH,
        )

    def columns(j):
        return pl.ds(pl.multiple_of(j * col, col), col)

    def product(k, e, j):
        rows = heads_out[...].reshape(-1, heads_out.shape[2])
        result = jnp.dot(rows, wo_v[:, columns(j)], preferred_element_type=F32).astype(BF16)
        result = result.reshape((batch, n_c, half, col))
        for core in range(n_c):
            for n in range(batch):
                part[k, e, j, core, n] = result[n, core]
        part_copy(k, e, j).start()

    def combine(k, e, j):
        part_copy(k, e, j).wait_recv()
        both = part[k, e, j, c].astype(F32) + part_in[k, e, j].astype(F32)
        summed[k, e, j] = both.astype(BF16)
        sum_copy(k, e, j).start()

    def products(k, e):
        attend(k, e)

        def step(j, carry):
            product(k, e, j)
            return carry

        lax.fori_loop(0, n_cols, step, 0)

    def combines(k, e, lo, hi):
        def step(j, carry):
            combine(k, e, j)
            return carry

        lax.fori_loop(lo, hi, step, 0)

    own = n_x - 1

    up = lane // (n_lanes // 2)

    def member(i):
        g = i % groups
        return i // groups, up * (1 + g) + (1 - up) * (n_lanes - 1 - g)

    behind = min(5, n_cols)

    def blend(k, e):
        attend(k, e)

        def step(j, carry):
            @pl.when(j < n_cols)
            def _():
                product(k, e, j)

            @pl.when(j >= behind)
            def _():
                combine(k, e, j - behind)

            return carry

        lax.fori_loop(0, n_cols + behind, step, 0)

    def some_products(k, e, lo, hi):
        def step(j, carry):
            product(k, e, j)
            return carry

        lax.fori_loop(lo, hi, step, 0)

    def relays(lo, hi):
        def step(i, carry):
            relay(*member(i))
            return carry

        lax.fori_loop(lo, hi, step, 0)

    def own_relays():
        for n in range(cap):
            relay(n, 0)

    def weights_here():
        for load in loads[2:]:
            load.wait()

    soon = cap // 2 * groups
    some = n_cols // 2

    def slot_step(i, carry):
        r, d = member(i)
        tok_copy(r, d).wait_recv()
        encode([(r, d)], lambda r, d: recv_tok[r, d])

        for n in range(ahead, cap):

            @pl.when(i == (n - 1) * groups - 1)
            def _():
                send_rank(n)

        if early:

            @pl.when(i == soon - 1)
            def _():
                own_relays()

            @pl.when(i == soon)
            def _():
                relays(0, 2)

            @pl.when(i == soon + 1)
            def _():
                relays(2, groups)
                weights_here()

            @pl.when(i == soon + 2)
            def _():
                relays(groups, soon)
                project(0)

            @pl.when(i == soon + 3)
            def _():
                project(1)

            @pl.when(i == soon + 4)
            def _():
                attend(0, 0)
                some_products(0, 0, 0, some)

            @pl.when(i == soon + 5)
            def _():
                combines(0, 0, 0, some // 2)
                some_products(0, 0, some, n_cols)
                combines(0, 0, some // 2, some)
                relays(soon, soon + groups)

        else:

            @pl.when(i == lag - 1)
            def _():
                own_relays()
                weights_here()

            @pl.when(i >= lag)
            def _():
                relays(i - lag, i - lag + 1)

            for n in range(cap - 1):

                @pl.when(i == (n + 1) * groups + lag - 1)
                def _():
                    project(n)

        return carry

    lax.fori_loop(0, total, slot_step, 0)
    if early:
        combines(0, 0, some, n_cols)
        relays(soon + groups, total)
        for n in range(cap // 2, cap):
            project(n)
    else:
        relays(total - lag, total)
        project(cap - 1)
    last = stages - 1
    for k in range(own):
        blend(k, last)
    for e in range(stages):
        products(own, e)

    def final_copy(j, n):
        rows = pl.ds(pl.multiple_of(n * span_len + c * half, half), half)
        return pltpu.make_async_remote_copy(
            src_ref=final_out.at[j, n], dst_ref=out_ref.at[rows, columns(j)],
            send_sem=final_send.at[0], recv_sem=final_recv.at[0],
            device_id={"rep": mate}, device_id_type=MESH,
        )

    def finish(j, carry):
        for e in range(stages):
            part_copy(own, e, j).wait_recv()
            total = part[own, e, j, c].astype(F32) + part_in[own, e, j].astype(F32)
            for k in range(own):
                sum_copy(k, e, j).wait_recv()
                total = total + summed_in[k, e, j].astype(F32)
            final[e * batch : (e + 1) * batch] = total.astype(BF16)
        for n in range(core_spans):
            first = x * chip_spans + n
            final_out[j, n] = final[slot_sm[first + mate * core_spans]]
            final_copy(j, n).start()
            rows = pl.ds(pl.multiple_of(n * span_len + c * half, half), half)
            out_ref[rows, columns(j)] = final[slot_sm[first + c * core_spans]]
        return carry

    lax.fori_loop(0, n_cols, finish, 0)
    for d in range(1, n_lanes):
        idx_copy(d).wait_send()
    for r in range(cap):
        toks_sent(r)
    sent(enc.at[:, :, pl.ds(0, n_x - 1)], x_send.at[0])
    sent(enc.at[:, :, pl.ds(0, n_x)], c_send.at[0])
    sent(part_in, part_send.at[0])
    sent(summed, sum_send.at[0])
    sent(final_out, final_send.at[0])
    pltpu.make_async_remote_copy(
        src_ref=final_out, dst_ref=final_out, send_sem=final_send.at[0], recv_sem=final_recv.at[0],
        device_id={"rep": mate}, device_id_type=MESH,
    ).wait_recv()


def shards(queries, span_states, store, entry_ids, owners, w_key, w_value, w_out):
    n_lanes, n_x, n_c = (lax.axis_size(name) for name in ("lanes", "heads", "rep"))
    spans, fanout = entry_ids.shape
    requests = spans * fanout
    cap = max(2, (requests + n_lanes - 1) // n_lanes)
    span_len = queries.shape[0] // spans
    tok_dev, width = store.shape[1:]
    tokens = tok_dev * n_x * n_c
    head_cols, model = w_out.shape
    out_rows = queries.shape[0] // (n_x * n_c)
    n_cols = 8
    core_spans = spans // (n_x * n_c)
    chip_spans = spans // n_x
    stages = 2 if early_spans(n_x, n_lanes, cap, spans, fanout) else 1
    batch = chip_spans // stages
    half = span_len // n_c
    col = model // n_cols
    lanes_wide = -(-(n_lanes * cap) // 128) * 128
    dma = pltpu.SemaphoreType.DMA
    hbm = pl.BlockSpec(memory_space=pl.ANY)
    smem = pl.BlockSpec(memory_space=pltpu.SMEM)
    return pl.pallas_call(
        functools.partial(fused, n_lanes, n_x, n_c, cap, n_cols),
        out_shape=pltpu.VMEM((out_rows, model), BF16),
        in_specs=[smem, smem] + [hbm] * 6,
        out_specs=pl.BlockSpec(memory_space=pltpu.VMEM),
        scratch_shapes=[
            pltpu.VMEM((spans, span_len, head_cols), BF16),
            pltpu.VMEM((spans, span_len, width), BF16),
            pltpu.VMEM(store.shape, BF16),
            pltpu.VMEM(w_key.shape, BF16),
            pltpu.VMEM(w_value.shape, BF16),
            pltpu.VMEM(w_out.shape, BF16),
            pltpu.VMEM((8, lanes_wide), jnp.int32),
            pltpu.VMEM((8, lanes_wide), jnp.int32),
            pltpu.SMEM((8, lanes_wide), jnp.int32),
            pltpu.SMEM((8, lanes_wide), jnp.int32),
            pltpu.SMEM((n_lanes, 8, lanes_wide), jnp.int32),
            pltpu.SMEM((requests,), jnp.int32),
            pltpu.SMEM((spans,), jnp.int32),
            pltpu.SMEM((spans,), jnp.int32),
            pltpu.VMEM((cap, n_lanes, tok_dev, width), BF16),
            pltpu.VMEM((cap, n_lanes, tok_dev, width), BF16),
            pltpu.VMEM((cap, n_lanes, n_x * n_c, tok_dev, width), BF16),
            pltpu.VMEM((cap, n_lanes, tokens, head_cols), BF16),
            pltpu.VMEM((cap, n_lanes, tokens, head_cols), BF16),
            pltpu.VMEM((batch, span_len, head_cols), BF16),
            pltpu.VMEM((n_x, stages, n_cols, n_c, batch, half, col), BF16),
            pltpu.VMEM((n_x, stages, n_cols, batch, half, col), BF16),
            pltpu.VMEM((n_x - 1, stages, n_cols, batch, half, col), BF16),
            pltpu.VMEM((n_x - 1, stages, n_cols, batch, half, col), BF16),
            pltpu.VMEM((chip_spans, half, col), BF16),
            pltpu.VMEM((n_cols, core_spans, half, col), BF16),
            dma((6,)),
            dma((2,)),
            dma((n_lanes,)),
            dma((n_lanes,)),
            dma((cap,)),
            dma((cap, n_lanes)),
            dma((1,)),
            dma((1,)),
            dma((cap, n_lanes, n_x - 1)),
            dma((cap,)),
            dma((1,)),
            dma((n_x, stages, n_cols)),
            dma((1,)),
            dma((n_x - 1, stages, n_cols)),
            dma((1,)),
            dma((1,)),
        ],
        compiler_params=pltpu.CompilerParams(
            collective_id=0, has_side_effects=True, vmem_limit_bytes=60000000
        ),
    )(
        owners.T,
        entry_ids.T,
        queries.reshape(spans, span_len, head_cols),
        span_states.reshape(spans, span_len, width),
        store,
        w_key,
        w_value,
        w_out,
    )


def solution(mesh):
    return jax.shard_map(
        shards,
        mesh=mesh,
        in_specs=(
            P(("groups", "lanes"), ("heads", "rep")),
            P(("groups", "lanes"), None),
            P(("groups", "lanes"), ("heads", "rep"), None),
            P(("groups", "lanes"), None),
            P(("groups", "lanes"), None),
            P(None, ("heads", "rep")),
            P(None, ("heads", "rep")),
            P(("heads", "rep"), None),
        ),
        out_specs=P(("groups", "lanes", "heads", "rep"), None),
        check_vma=False,
    )
```

```python
import functools
import itertools

import jax
import jax.numpy as jnp
from jax import lax
from jax.experimental import pallas as pl
from jax.experimental.pallas import tpu as pltpu
from jax.sharding import PartitionSpec as P

HD = 128
ENCODER_HEAD_DIM = 128
MESH = pl.DeviceIdType.MESH
F32 = jnp.float32
BF16 = jnp.bfloat16


def softmax_parts(parts):
    top = functools.reduce(jnp.maximum, [jnp.max(p, axis=-1, keepdims=True) for p in parts])
    exps = [jnp.exp(p - top) for p in parts]
    total = functools.reduce(jnp.add, [jnp.sum(e, axis=-1, keepdims=True) for e in exps])
    inv = 1.0 / total
    return [(e * inv).astype(BF16) for e in exps]


def dot_t(a, b):
    return lax.dot_general(a, b, (((1,), (1,)), ((), ())), preferred_element_type=F32)


def early_spans(n_x, n_lanes, cap, spans, fanout):
    whole = n_x == 2 and cap == n_lanes == 4 and fanout == 2 and spans == 2 * n_lanes
    return spans // n_x // 2 if whole else 0


def fused(
    n_lanes, n_x, n_c, cap, n_cols,
    owner_ref, entry_ref, query_hbm, states_hbm, store_hbm, wk_hbm, wv_hbm, wo_hbm,
    out_ref,
    query_v, states_v, store_v, wk_v, wv_v, wo_v,
    table, span_table, span_sm, own_sm, got_sm, rank_sm, virtual_sm, slot_sm,
    send_tok, recv_tok, enc, keys, values, heads_out,
    part, part_in, summed, summed_in, final, final_out,
    load_sem, local_sem, idx_send, idx_recv, tok_sends, tok_recvs, x_send, c_send, x_recvs, c_recvs,
    part_send, part_recv, own_recv, sum_send, sum_recv, early_recv, final_send, final_recv,
):
    lane = lax.axis_index("lanes")
    x = lax.axis_index("heads")
    c = lax.axis_index("rep")
    mate = n_c - 1 - c
    fanout, spans = owner_ref.shape
    requests = spans * fanout
    width = store_v.shape[2]
    span_len = query_v.shape[1]
    chip_spans = spans // n_x
    core_spans = chip_spans // n_c
    col = wo_v.shape[1] // n_cols
    half = span_len // n_c
    quarter = x * n_c + c
    early = early_spans(n_x, n_lanes, cap, spans, fanout)
    stages = part.shape[1]
    own = n_x - 1
    last = stages - 1
    batch = chip_spans // stages

    loads = [
        pltpu.make_async_copy(src, dst, load_sem.at[i])
        for i, (src, dst) in enumerate(
            (
                (store_hbm, store_v),
                (states_hbm, states_v),
                (wk_hbm, wk_v),
                (wv_hbm, wv_v),
                (query_hbm, query_v),
                (wo_hbm, wo_v),
            )
        )
    ]
    for load in loads[:2]:
        load.start()

    barrier = pltpu.get_barrier_semaphore()
    for d in range(1, n_lanes):
        pl.semaphore_signal(barrier, inc=1, device_id={"lanes": lax.rem(lane + d, n_lanes)}, device_id_type=MESH)
    for d in range(1, n_x):
        pl.semaphore_signal(barrier, inc=1, device_id={"heads": lax.rem(x + d, n_x)}, device_id_type=MESH)
    pl.semaphore_signal(barrier, inc=1, device_id={"rep": mate}, device_id_type=MESH)

    owner = [owner_ref[j % fanout, j // fanout] for j in range(requests)]
    ranks = []
    if early:
        word = [
            sum(jnp.where(owner[s * fanout + f] == o, 1 << (4 * o), 0) for f in range(fanout) for o in range(n_lanes))
            for s in range(spans)
        ]
        target = sum((cap // 2) << (4 * o) for o in range(n_lanes))
        chosen = list(itertools.combinations(range(chip_spans), early))
        sums = [[sum(word[h * chip_spans + s] for s in some) for some in chosen] for h in range(n_x)]
        mask = jnp.int32(0)
        for a, some in enumerate(chosen):
            for b, others in enumerate(chosen):
                bits = sum(1 << s for s in some) + sum(1 << (chip_spans + s) for s in others)
                mask = jnp.where(sums[0][a] + sums[1][b] == target, bits, mask)
        first, later = jnp.int32(0), jnp.int32(target)
        slot = []
        for s in range(spans):
            if s % chip_spans == 0:
                n_first, n_later = jnp.int32(0), jnp.int32(early)
            taken = ((mask >> s) & 1) == 1
            ahead = jnp.where(taken, first, later)
            for f in range(fanout):
                ranks.append(
                    sum(jnp.where(owner[s * fanout + f] == o, (ahead >> (4 * o)) & 15, 0) for o in range(n_lanes))
                )
            first, later = first + jnp.where(taken, word[s], 0), later + jnp.where(taken, 0, word[s])
            slot.append(jnp.where(taken, n_first, n_later))
            n_first, n_later = n_first + jnp.where(taken, 1, 0), n_later + jnp.where(taken, 0, 1)
        for s in range(spans):
            base = s // chip_spans * chip_spans
            slot_sm[s] = jnp.minimum(slot[s], chip_spans - 1)
            virtual_sm[s] = sum(jnp.where(slot[base + i] == s - base, base + i, 0) for i in range(chip_spans))
    else:
        for j in range(requests):
            ranks.append(sum((owner[i] == owner[j]).astype(jnp.int32) for i in range(j)) + jnp.int32(0))
        for s in range(spans):
            slot_sm[s] = s % chip_spans
            virtual_sm[s] = s
    place = lax.broadcasted_iota(jnp.int32, table.shape, 1)
    entries = jnp.zeros(table.shape, jnp.int32)
    whose = jnp.zeros(table.shape, jnp.int32)
    for j, rank in enumerate(ranks):
        rank_sm[j] = jnp.minimum(rank, cap - 1)
        hit = place == owner[j] * cap + rank
        entries = jnp.where(hit, entry_ref[j % fanout, j // fanout], entries)
        whose = jnp.where(hit, j // fanout, whose)
    table[...] = entries
    span_table[...] = whose
    pl.semaphore_wait(barrier, n_lanes + n_x - 1)

    def idx_copy(d):
        return pltpu.make_async_remote_copy(
            src_ref=table, dst_ref=got_sm.at[lane], send_sem=idx_send.at[0], recv_sem=idx_recv.at[d - 1],
            device_id={"lanes": lax.rem(lane + d, n_lanes)}, device_id_type=MESH,
        )

    for d in range(1, n_lanes):
        idx_copy(d).start()
    to_sm = pltpu.make_async_copy(span_table, span_sm, local_sem.at[0])
    to_sm.start()
    own_to_sm = pltpu.make_async_copy(table, own_sm, local_sem.at[1])
    own_to_sm.start()
    to_sm.wait()
    own_to_sm.wait()
    loads[0].wait()
    loads[1].wait()
    for load in loads[2:]:
        load.start()

    def tok_copy(r, d):
        return pltpu.make_async_remote_copy(
            src_ref=send_tok.at[r, d], dst_ref=recv_tok.at[r, d],
            send_sem=tok_sends.at[r], recv_sem=tok_recvs.at[r, d - 1],
            device_id={"lanes": lax.rem(lane + d, n_lanes)}, device_id_type=MESH,
        )

    def sent(ref, sem):
        pltpu.make_async_remote_copy(
            src_ref=ref, dst_ref=ref, send_sem=sem, recv_sem=sem, device_id={"rep": mate}, device_id_type=MESH
        ).wait_send()

    def toks_sent(r):
        sent(send_tok.at[r, pl.ds(1, n_lanes - 1)], tok_sends.at[r])

    def send_one(r, d):
        who = lax.rem(lane + d, n_lanes)
        send_tok[r, d] = store_v[got_sm[who, 0, lane * cap + r]]
        tok_copy(r, d).start()

    def send_rank(r):
        def one(d, carry):
            send_one(r, d)
            return carry

        lax.fori_loop(1, n_lanes, one, 0)

    def x_copy(r, s, d):
        return pltpu.make_async_remote_copy(
            src_ref=enc.at[r, s, quarter], dst_ref=enc.at[r, s, quarter],
            send_sem=x_send.at[0], recv_sem=x_recvs.at[r, s, d - 1],
            device_id={"heads": lax.rem(x + d, n_x)}, device_id_type=MESH,
        )

    def c_copy(r, s, block):
        return pltpu.make_async_remote_copy(
            src_ref=enc.at[r, s, block], dst_ref=enc.at[r, s, block],
            send_sem=c_send.at[0], recv_sem=c_recvs.at[r],
            device_id={"rep": mate}, device_id_type=MESH,
        )

    def source(d):
        return lax.rem(lane - d + n_lanes, n_lanes)

    def encode(group, fetch):
        tokens = [fetch(r, d) for r, d in group]
        states = [states_v[span_sm[0, source(d) * cap + r]] for r, d in group]
        heads = [
            (n, slice(h * ENCODER_HEAD_DIM, (h + 1) * ENCODER_HEAD_DIM))
            for n in range(len(group))
            for h in range(width // ENCODER_HEAD_DIM)
        ]
        logits = [dot_t(tokens[n][:, cols], states[n][:, cols]) * ENCODER_HEAD_DIM ** (-0.5) for n, cols in heads]
        weights = [softmax_parts([logit])[0] for logit in logits]
        mixed = [
            jnp.dot(weight, states[n][:, cols], preferred_element_type=F32) for weight, (n, cols) in zip(weights, heads)
        ]
        for mix, (n, cols) in zip(mixed, heads):
            r, d = group[n]
            enc[r, source(d), quarter, :, cols] = (tokens[n][:, cols].astype(F32) + mix).astype(BF16)
        for r, d in group:
            s = source(d)
            for k in range(1, n_x):
                x_copy(r, s, k).start()
            c_copy(r, s, quarter).start()

    def relay(r, d):
        s = source(d)
        for k in range(1, n_x):
            block = lax.rem(x - k + n_x, n_x) * n_c + c
            pltpu.make_async_remote_copy(
                src_ref=enc.at[r, s, block], dst_ref=enc.at[r, s, block],
                send_sem=x_send.at[0], recv_sem=x_recvs.at[r, s, k - 1],
                device_id={"rep": mate}, device_id_type=MESH,
            ).wait_recv()
            c_copy(r, s, block).start()

    encode([(r, 0) for r in range(cap)], lambda r, d: store_v[own_sm[0, lane * cap + r]])
    ahead = min(2, cap)
    for d in sorted(range(1, n_lanes), key=lambda d: min(d, n_lanes - d)):
        idx_copy(d).wait_recv()
        send_one(0, n_lanes - d)
    for r in range(1, ahead):
        send_rank(r)
    groups = n_lanes - 1
    total = cap * groups
    lag = min(3, groups)
    lane_chunk = min(n_lanes, 4)

    def settle(r):
        ref = enc.at[r, :, pl.ds(0, n_x)]
        pltpu.make_async_remote_copy(
            src_ref=ref, dst_ref=ref, send_sem=c_send.at[0], recv_sem=c_recvs.at[r],
            device_id={"rep": mate}, device_id_type=MESH,
        ).wait_recv()

    def project(r):
        settle(r)

        def chunk(g, carry):
            some = pl.ds(g * lane_chunk, lane_chunk)
            rows = enc[r, some].reshape(-1, width)
            for weight, target in ((wk_v, keys), (wv_v, values)):
                result = jnp.dot(rows, weight[...], preferred_element_type=F32).astype(BF16)
                target[r, some] = result.reshape((lane_chunk,) + target.shape[2:])
            return carry

        lax.fori_loop(0, n_lanes // lane_chunk, chunk, 0)

    def attend(k, e):
        first = lax.rem(x + k + 1, n_x) * chip_spans + e * batch
        which = [virtual_sm[first + n] for n in range(batch)]
        slots = [[(rank_sm[s * fanout + f], owner_ref[f, s]) for f in range(fanout)] for s in which]
        heads = [(n, slice(h * HD, (h + 1) * HD)) for n in range(batch) for h in range(query_v.shape[2] // HD)]
        logits = [
            [dot_t(query_v[which[n], :, cols], keys[r, o, :, cols]) * HD ** (-0.5) for r, o in slots[n]]
            for n, cols in heads
        ]
        weights = [softmax_parts(parts) for parts in logits]
        mixed = [
            functools.reduce(
                jnp.add,
                [
                    jnp.dot(w, values[r, o, :, cols], preferred_element_type=F32)
                    for w, (r, o) in zip(parts, slots[n])
                ],
            )
            for parts, (n, cols) in zip(weights, heads)
        ]
        for mix, (n, cols) in zip(mixed, heads):
            heads_out[n, :, cols] = mix.astype(BF16)

    def part_copy(k, e, j):
        return pltpu.make_async_remote_copy(
            src_ref=part.at[k, e, j, mate], dst_ref=part_in.at[k, e, j],
            send_sem=part_send.at[0], recv_sem=part_recv.at[k, e, j] if k < own else own_recv.at[e],
            device_id={"rep": mate}, device_id_type=MESH,
        )

    def sum_copy(k, e, j):
        return pltpu.make_async_remote_copy(
            src_ref=summed.at[k, e, j], dst_ref=summed_in.at[k, e, j],
            send_sem=sum_send.at[0], recv_sem=sum_recv.at[k, j] if e == last else early_recv.at[k],
            device_id={"heads": lax.rem(x + k + 1, n_x)}, device_id_type=MESH,
        )

    def columns(j):
        return pl.ds(pl.multiple_of(j * col, col), col)

    def product(k, e, j):
        rows = heads_out[...].reshape(-1, heads_out.shape[2])
        result = jnp.dot(rows, wo_v[:, columns(j)], preferred_element_type=F32).astype(BF16)
        result = result.reshape((batch, n_c, half, col))
        for core in range(n_c):
            for n in range(batch):
                part[k, e, j, core, n] = result[n, core]
        part_copy(k, e, j).start()

    def combine(k, e, j):
        part_copy(k, e, j).wait_recv()
        both = part[k, e, j, c].astype(F32) + part_in[k, e, j].astype(F32)
        summed[k, e, j] = both.astype(BF16)
        sum_copy(k, e, j).start()

    def products(k, e):
        attend(k, e)

        def step(j, carry):
            product(k, e, j)
            return carry

        lax.fori_loop(0, n_cols, step, 0)

    def combines(k, e, lo, hi):
        def step(j, carry):
            combine(k, e, j)
            return carry

        lax.fori_loop(lo, hi, step, 0)


    up = lane // (n_lanes // 2)

    def member(i):
        g = i % groups
        return i // groups, up * (1 + g) + (1 - up) * (n_lanes - 1 - g)

    behind = min(5, n_cols)

    def blend(k, e):
        attend(k, e)

        def step(j, carry):
            @pl.when(j < n_cols)
            def _():
                product(k, e, j)

            @pl.when(j >= behind)
            def _():
                combine(k, e, j - behind)

            return carry

        lax.fori_loop(0, n_cols + behind, step, 0)

    def some_products(k, e, lo, hi):
        def step(j, carry):
            product(k, e, j)
            return carry

        lax.fori_loop(lo, hi, step, 0)

    def relays(lo, hi):
        def step(i, carry):
            relay(*member(i))
            return carry

        lax.fori_loop(lo, hi, step, 0)

    def own_relays():
        for n in range(cap):
            relay(n, 0)

    def weights_here():
        for load in loads[2:]:
            load.wait()

    soon = cap // 2 * groups
    some = n_cols // 2

    def slot_step(i, carry):
        r, d = member(i)
        tok_copy(r, d).wait_recv()
        encode([(r, d)], lambda r, d: recv_tok[r, d])

        for n in range(ahead, cap):

            @pl.when(i == (n - 1) * groups - 1)
            def _():
                send_rank(n)

        if early:

            @pl.when(i == soon - 1)
            def _():
                own_relays()

            @pl.when(i == soon)
            def _():
                relays(0, 2)

            @pl.when(i == soon + 1)
            def _():
                relays(2, groups)
                weights_here()

            @pl.when(i == soon + 2)
            def _():
                relays(groups, soon)
                project(0)

            @pl.when(i == soon + 3)
            def _():
                project(1)

            @pl.when(i == soon + 4)
            def _():
                attend(0, 0)

            @pl.when(i == soon + 5)
            def _():
                some_products(0, 0, 0, some)
                combines(0, 0, 0, 1)
                some_products(0, 0, some, n_cols)
                combines(0, 0, 1, 4)
                relays(soon, soon + groups)

        else:

            @pl.when(i == lag - 1)
            def _():
                own_relays()
                weights_here()

            @pl.when(i >= lag)
            def _():
                relays(i - lag, i - lag + 1)

            for n in range(cap - 1):

                @pl.when(i == (n + 1) * groups + lag - 1)
                def _():
                    project(n)

        return carry

    lax.fori_loop(0, total, slot_step, 0)
    if early:
        combines(0, 0, 4, n_cols)
        relays(soon + groups, total)
        for n in range(cap // 2, cap):
            project(n)
    else:
        relays(total - lag, total)
        project(cap - 1)
    for k in range(own):
        blend(k, last)
    for e in range(stages):
        products(own, e)

    def final_copy(j, n):
        rows = pl.ds(pl.multiple_of(n * span_len + c * half, half), half)
        return pltpu.make_async_remote_copy(
            src_ref=final_out.at[j, n], dst_ref=out_ref.at[rows, columns(j)],
            send_sem=final_send.at[0], recv_sem=final_recv.at[0],
            device_id={"rep": mate}, device_id_type=MESH,
        )

    def finish(j, carry):
        for e in range(stages):
            total = part[own, e, j, c].astype(F32) + part_in[own, e, j].astype(F32)
            for k in range(own):
                if e == last:
                    sum_copy(k, e, j).wait_recv()
                total = total + summed_in[k, e, j].astype(F32)
            final[e * batch : (e + 1) * batch] = total.astype(BF16)
        for n in range(core_spans):
            first = x * chip_spans + n
            final_out[j, n] = final[slot_sm[first + mate * core_spans]]
            final_copy(j, n).start()
            rows = pl.ds(pl.multiple_of(n * span_len + c * half, half), half)
            out_ref[rows, columns(j)] = final[slot_sm[first + c * core_spans]]
        return carry

    def arrived(ref, sem):
        pltpu.make_async_remote_copy(
            src_ref=ref, dst_ref=ref, send_sem=sem, recv_sem=sem, device_id={"rep": mate}, device_id_type=MESH
        ).wait_recv()

    for e in range(stages):
        arrived(part_in.at[own, e], own_recv.at[e])
    for k in range(own if last else 0):
        arrived(summed_in.at[k, 0], early_recv.at[k])
    lax.fori_loop(0, n_cols, finish, 0)
    sent(got_sm.at[pl.ds(0, n_lanes - 1)], idx_send.at[0])
    for r in range(cap):
        toks_sent(r)
    sent(enc.at[:, :, pl.ds(0, n_x - 1)], x_send.at[0])
    sent(enc.at[:, :, pl.ds(0, n_x)], c_send.at[0])
    sent(part_in, part_send.at[0])
    sent(summed, sum_send.at[0])
    sent(final_out, final_send.at[0])
    pltpu.make_async_remote_copy(
        src_ref=final_out, dst_ref=final_out, send_sem=final_send.at[0], recv_sem=final_recv.at[0],
        device_id={"rep": mate}, device_id_type=MESH,
    ).wait_recv()


def shards(queries, span_states, store, entry_ids, owners, w_key, w_value, w_out):
    n_lanes, n_x, n_c = (lax.axis_size(name) for name in ("lanes", "heads", "rep"))
    spans, fanout = entry_ids.shape
    requests = spans * fanout
    cap = max(2, (requests + n_lanes - 1) // n_lanes)
    span_len = queries.shape[0] // spans
    tok_dev, width = store.shape[1:]
    tokens = tok_dev * n_x * n_c
    head_cols, model = w_out.shape
    out_rows = queries.shape[0] // (n_x * n_c)
    n_cols = 8
    core_spans = spans // (n_x * n_c)
    chip_spans = spans // n_x
    stages = 2 if early_spans(n_x, n_lanes, cap, spans, fanout) else 1
    batch = chip_spans // stages
    half = span_len // n_c
    col = model // n_cols
    lanes_wide = -(-(n_lanes * cap) // 128) * 128
    dma = pltpu.SemaphoreType.DMA
    hbm = pl.BlockSpec(memory_space=pl.ANY)
    smem = pl.BlockSpec(memory_space=pltpu.SMEM)
    return pl.pallas_call(
        functools.partial(fused, n_lanes, n_x, n_c, cap, n_cols),
        out_shape=pltpu.VMEM((out_rows, model), BF16),
        in_specs=[smem, smem] + [hbm] * 6,
        out_specs=pl.BlockSpec(memory_space=pltpu.VMEM),
        scratch_shapes=[
            pltpu.VMEM((spans, span_len, head_cols), BF16),
            pltpu.VMEM((spans, span_len, width), BF16),
            pltpu.VMEM(store.shape, BF16),
            pltpu.VMEM(w_key.shape, BF16),
            pltpu.VMEM(w_value.shape, BF16),
            pltpu.VMEM(w_out.shape, BF16),
            pltpu.VMEM((8, lanes_wide), jnp.int32),
            pltpu.VMEM((8, lanes_wide), jnp.int32),
            pltpu.SMEM((8, lanes_wide), jnp.int32),
            pltpu.SMEM((8, lanes_wide), jnp.int32),
            pltpu.SMEM((n_lanes, 8, lanes_wide), jnp.int32),
            pltpu.SMEM((requests,), jnp.int32),
            pltpu.SMEM((spans,), jnp.int32),
            pltpu.SMEM((spans,), jnp.int32),
            pltpu.VMEM((cap, n_lanes, tok_dev, width), BF16),
            pltpu.VMEM((cap, n_lanes, tok_dev, width), BF16),
            pltpu.VMEM((cap, n_lanes, n_x * n_c, tok_dev, width), BF16),
            pltpu.VMEM((cap, n_lanes, tokens, head_cols), BF16),
            pltpu.VMEM((cap, n_lanes, tokens, head_cols), BF16),
            pltpu.VMEM((batch, span_len, head_cols), BF16),
            pltpu.VMEM((n_x, stages, n_cols, n_c, batch, half, col), BF16),
            pltpu.VMEM((n_x, stages, n_cols, batch, half, col), BF16),
            pltpu.VMEM((n_x - 1, stages, n_cols, batch, half, col), BF16),
            pltpu.VMEM((n_x - 1, stages, n_cols, batch, half, col), BF16),
            pltpu.VMEM((chip_spans, half, col), BF16),
            pltpu.VMEM((n_cols, core_spans, half, col), BF16),
            dma((6,)),
            dma((2,)),
            dma((1,)),
            dma((n_lanes - 1,)),
            dma((cap,)),
            dma((cap, n_lanes - 1)),
            dma((1,)),
            dma((1,)),
            dma((cap, n_lanes, n_x - 1)),
            dma((cap,)),
            dma((1,)),
            dma((n_x - 1, stages, n_cols)),
            dma((stages,)),
            dma((1,)),
            dma((n_x - 1, n_cols)),
            dma((n_x - 1,)),
            dma((1,)),
            dma((1,)),
        ],
        compiler_params=pltpu.CompilerParams(
            collective_id=0, has_side_effects=True, vmem_limit_bytes=60000000
        ),
    )(
        owners.T,
        entry_ids.T,
        queries.reshape(spans, span_len, head_cols),
        span_states.reshape(spans, span_len, width),
        store,
        w_key,
        w_value,
        w_out,
    )


def solution(mesh):
    return jax.shard_map(
        shards,
        mesh=mesh,
        in_specs=(
            P(("groups", "lanes"), ("heads", "rep")),
            P(("groups", "lanes"), None),
            P(("groups", "lanes"), ("heads", "rep"), None),
            P(("groups", "lanes"), None),
            P(("groups", "lanes"), None),
            P(None, ("heads", "rep")),
            P(None, ("heads", "rep")),
            P(("heads", "rep"), None),
        ),
        out_specs=P(("groups", "lanes", "heads", "rep"), None),
        check_vma=False,
    )
```

```python
import functools
import itertools

import jax
import jax.numpy as jnp
from jax import lax
from jax.experimental import pallas as pl
from jax.experimental.pallas import tpu as pltpu
from jax.sharding import PartitionSpec as P

HD = 128
ENCODER_HEAD_DIM = 128
MESH = pl.DeviceIdType.MESH
F32 = jnp.float32
BF16 = jnp.bfloat16


def softmax_parts(parts):
    top = functools.reduce(jnp.maximum, [jnp.max(p, axis=-1, keepdims=True) for p in parts])
    exps = [jnp.exp(p - top) for p in parts]
    total = functools.reduce(jnp.add, [jnp.sum(e, axis=-1, keepdims=True) for e in exps])
    inv = 1.0 / total
    return [(e * inv).astype(BF16) for e in exps]


def dot_t(a, b):
    return lax.dot_general(a, b, (((1,), (1,)), ((), ())), preferred_element_type=F32)


def early_spans(n_x, n_lanes, cap, spans, fanout):
    whole = n_x == 2 and cap == n_lanes == 4 and fanout == 2 and spans == 2 * n_lanes
    return spans // n_x // 2 if whole else 0


def fused(
    n_lanes, n_x, n_c, cap, n_cols,
    owner_ref, entry_ref, query_hbm, states_hbm, store_hbm, wk_hbm, wv_hbm, wo_hbm,
    out_ref,
    query_v, states_v, store_v, wk_v, wv_v, wo_v,
    table, span_table, span_sm, own_sm, got_sm, rank_sm, virtual_sm, slot_sm,
    send_tok, recv_tok, enc, keys, values, heads_out,
    part, part_in, summed, summed_in, final, final_out,
    load_sem, local_sem, idx_send, idx_recv, tok_sends, tok_recvs, x_send, c_send, x_recvs, c_recvs,
    part_send, part_recv, own_recv, sum_send, sum_recv, early_recv, final_send, final_recv,
):
    lane = lax.axis_index("lanes")
    x = lax.axis_index("heads")
    c = lax.axis_index("rep")
    mate = n_c - 1 - c
    fanout, spans = owner_ref.shape
    requests = spans * fanout
    width = store_v.shape[2]
    span_len = query_v.shape[1]
    chip_spans = spans // n_x
    core_spans = chip_spans // n_c
    col = wo_v.shape[1] // n_cols
    half = span_len // n_c
    quarter = x * n_c + c
    early = early_spans(n_x, n_lanes, cap, spans, fanout)
    stages = part.shape[1]
    own = n_x - 1
    last = stages - 1
    batch = chip_spans // stages

    loads = [
        pltpu.make_async_copy(src, dst, load_sem.at[i])
        for i, (src, dst) in enumerate(
            (
                (store_hbm, store_v),
                (states_hbm, states_v),
                (wk_hbm, wk_v),
                (wv_hbm, wv_v),
                (query_hbm, query_v),
                (wo_hbm, wo_v),
            )
        )
    ]
    for load in loads[:2]:
        load.start()

    barrier = pltpu.get_barrier_semaphore()
    for d in range(1, n_lanes):
        pl.semaphore_signal(barrier, inc=1, device_id={"lanes": lax.rem(lane + d, n_lanes)}, device_id_type=MESH)
    for d in range(1, n_x):
        pl.semaphore_signal(barrier, inc=1, device_id={"heads": lax.rem(x + d, n_x)}, device_id_type=MESH)
    pl.semaphore_signal(barrier, inc=1, device_id={"rep": mate}, device_id_type=MESH)

    owner = [owner_ref[j % fanout, j // fanout] for j in range(requests)]
    ranks = []
    if early:
        word = [
            sum(jnp.where(owner[s * fanout + f] == o, 1 << (4 * o), 0) for f in range(fanout) for o in range(n_lanes))
            for s in range(spans)
        ]
        target = sum((cap // 2) << (4 * o) for o in range(n_lanes))
        chosen = list(itertools.combinations(range(chip_spans), early))
        sums = [[sum(word[h * chip_spans + s] for s in some) for some in chosen] for h in range(n_x)]
        mask = jnp.int32(0)
        for a, some in enumerate(chosen):
            for b, others in enumerate(chosen):
                bits = sum(1 << s for s in some) + sum(1 << (chip_spans + s) for s in others)
                mask = jnp.where(sums[0][a] + sums[1][b] == target, bits, mask)
        first, later = jnp.int32(0), jnp.int32(target)
        slot = []
        for s in range(spans):
            if s % chip_spans == 0:
                n_first, n_later = jnp.int32(0), jnp.int32(early)
            taken = ((mask >> s) & 1) == 1
            ahead = jnp.where(taken, first, later)
            for f in range(fanout):
                ranks.append(
                    sum(jnp.where(owner[s * fanout + f] == o, (ahead >> (4 * o)) & 15, 0) for o in range(n_lanes))
                )
            first, later = first + jnp.where(taken, word[s], 0), later + jnp.where(taken, 0, word[s])
            slot.append(jnp.where(taken, n_first, n_later))
            n_first, n_later = n_first + jnp.where(taken, 1, 0), n_later + jnp.where(taken, 0, 1)
        for s in range(spans):
            base = s // chip_spans * chip_spans
            slot_sm[s] = jnp.minimum(slot[s], chip_spans - 1)
            virtual_sm[s] = sum(jnp.where(slot[base + i] == s - base, base + i, 0) for i in range(chip_spans))
    else:
        for j in range(requests):
            ranks.append(sum((owner[i] == owner[j]).astype(jnp.int32) for i in range(j)) + jnp.int32(0))
        for s in range(spans):
            slot_sm[s] = s % chip_spans
            virtual_sm[s] = s
    place = lax.broadcasted_iota(jnp.int32, table.shape, 1)
    entries = jnp.zeros(table.shape, jnp.int32)
    whose = jnp.zeros(table.shape, jnp.int32)
    for j, rank in enumerate(ranks):
        rank_sm[j] = jnp.minimum(rank, cap - 1)
        hit = place == owner[j] * cap + rank
        entries = jnp.where(hit, entry_ref[j % fanout, j // fanout], entries)
        whose = jnp.where(hit, j // fanout, whose)
    table[...] = entries
    span_table[...] = whose
    pl.semaphore_wait(barrier, n_lanes + n_x - 1)

    def idx_copy(d):
        return pltpu.make_async_remote_copy(
            src_ref=table, dst_ref=got_sm.at[lane], send_sem=idx_send.at[0], recv_sem=idx_recv.at[d - 1],
            device_id={"lanes": lax.rem(lane + d, n_lanes)}, device_id_type=MESH,
        )

    for d in range(1, n_lanes):
        idx_copy(d).start()
    to_sm = pltpu.make_async_copy(span_table, span_sm, local_sem.at[0])
    to_sm.start()
    own_to_sm = pltpu.make_async_copy(table, own_sm, local_sem.at[1])
    own_to_sm.start()
    to_sm.wait()
    own_to_sm.wait()
    loads[0].wait()
    loads[1].wait()
    for load in loads[2:]:
        load.start()

    def tok_copy(r, d):
        return pltpu.make_async_remote_copy(
            src_ref=send_tok.at[r, d], dst_ref=recv_tok.at[r, d],
            send_sem=tok_sends.at[r], recv_sem=tok_recvs.at[r, d - 1],
            device_id={"lanes": lax.rem(lane + d, n_lanes)}, device_id_type=MESH,
        )

    def sent(ref, sem):
        pltpu.make_async_remote_copy(
            src_ref=ref, dst_ref=ref, send_sem=sem, recv_sem=sem, device_id={"rep": mate}, device_id_type=MESH
        ).wait_send()

    def toks_sent(r):
        sent(send_tok.at[r, pl.ds(1, n_lanes - 1)], tok_sends.at[r])

    def send_one(r, d):
        who = lax.rem(lane + d, n_lanes)
        send_tok[r, d] = store_v[got_sm[who, 0, lane * cap + r]]
        tok_copy(r, d).start()

    def send_rank(r):
        def one(d, carry):
            send_one(r, d)
            return carry

        lax.fori_loop(1, n_lanes, one, 0)

    def x_copy(r, s, d):
        return pltpu.make_async_remote_copy(
            src_ref=enc.at[r, s, quarter], dst_ref=enc.at[r, s, quarter],
            send_sem=x_send.at[0], recv_sem=x_recvs.at[r, s, d - 1],
            device_id={"heads": lax.rem(x + d, n_x)}, device_id_type=MESH,
        )

    def c_copy(r, s, block):
        return pltpu.make_async_remote_copy(
            src_ref=enc.at[r, s, block], dst_ref=enc.at[r, s, block],
            send_sem=c_send.at[0], recv_sem=c_recvs.at[r],
            device_id={"rep": mate}, device_id_type=MESH,
        )

    def source(d):
        return lax.rem(lane - d + n_lanes, n_lanes)

    def encode(group, fetch):
        tokens = [fetch(r, d) for r, d in group]
        states = [states_v[span_sm[0, source(d) * cap + r]] for r, d in group]
        heads = [
            (n, slice(h * ENCODER_HEAD_DIM, (h + 1) * ENCODER_HEAD_DIM))
            for n in range(len(group))
            for h in range(width // ENCODER_HEAD_DIM)
        ]
        logits = [dot_t(tokens[n][:, cols], states[n][:, cols]) * ENCODER_HEAD_DIM ** (-0.5) for n, cols in heads]
        weights = [softmax_parts([logit])[0] for logit in logits]
        mixed = [
            jnp.dot(weight, states[n][:, cols], preferred_element_type=F32) for weight, (n, cols) in zip(weights, heads)
        ]
        for mix, (n, cols) in zip(mixed, heads):
            r, d = group[n]
            enc[r, source(d), quarter, :, cols] = (tokens[n][:, cols].astype(F32) + mix).astype(BF16)
        for r, d in group:
            s = source(d)
            for k in range(1, n_x):
                x_copy(r, s, k).start()
            c_copy(r, s, quarter).start()

    def relay(r, d):
        s = source(d)
        for k in range(1, n_x):
            block = lax.rem(x - k + n_x, n_x) * n_c + c
            pltpu.make_async_remote_copy(
                src_ref=enc.at[r, s, block], dst_ref=enc.at[r, s, block],
                send_sem=x_send.at[0], recv_sem=x_recvs.at[r, s, k - 1],
                device_id={"rep": mate}, device_id_type=MESH,
            ).wait_recv()
            c_copy(r, s, block).start()

    encode([(r, 0) for r in range(cap)], lambda r, d: store_v[own_sm[0, lane * cap + r]])
    ahead = min(2, cap)
    for d in sorted(range(1, n_lanes), key=lambda d: min(d, n_lanes - d)):
        idx_copy(d).wait_recv()
        send_one(0, n_lanes - d)
    for r in range(1, ahead):
        send_rank(r)
    groups = n_lanes - 1
    total = cap * groups
    lag = min(3, groups)
    lane_chunk = min(n_lanes, 4)

    def settle(r):
        ref = enc.at[r, :, pl.ds(0, n_x)]
        pltpu.make_async_remote_copy(
            src_ref=ref, dst_ref=ref, send_sem=c_send.at[0], recv_sem=c_recvs.at[r],
            device_id={"rep": mate}, device_id_type=MESH,
        ).wait_recv()

    def project(r):
        settle(r)

        def chunk(g, carry):
            some = pl.ds(g * lane_chunk, lane_chunk)
            rows = enc[r, some].reshape(-1, width)
            for weight, target in ((wk_v, keys), (wv_v, values)):
                result = jnp.dot(rows, weight[...], preferred_element_type=F32).astype(BF16)
                target[r, some] = result.reshape((lane_chunk,) + target.shape[2:])
            return carry

        lax.fori_loop(0, n_lanes // lane_chunk, chunk, 0)

    def attend(k, e):
        first = lax.rem(x + k + 1, n_x) * chip_spans + e * batch
        which = [virtual_sm[first + n] for n in range(batch)]
        slots = [[(rank_sm[s * fanout + f], owner_ref[f, s]) for f in range(fanout)] for s in which]
        heads = [(n, slice(h * HD, (h + 1) * HD)) for n in range(batch) for h in range(query_v.shape[2] // HD)]
        logits = [
            [dot_t(query_v[which[n], :, cols], keys[r, o, :, cols]) * HD ** (-0.5) for r, o in slots[n]]
            for n, cols in heads
        ]
        weights = [softmax_parts(parts) for parts in logits]
        mixed = [
            functools.reduce(
                jnp.add,
                [
                    jnp.dot(w, values[r, o, :, cols], preferred_element_type=F32)
                    for w, (r, o) in zip(parts, slots[n])
                ],
            )
            for parts, (n, cols) in zip(weights, heads)
        ]
        for mix, (n, cols) in zip(mixed, heads):
            heads_out[n, :, cols] = mix.astype(BF16)

    def part_copy(k, e, j):
        return pltpu.make_async_remote_copy(
            src_ref=part.at[k, e, j, mate], dst_ref=part_in.at[k, e, j],
            send_sem=part_send.at[0], recv_sem=part_recv.at[k, e, j] if k < own else own_recv.at[e],
            device_id={"rep": mate}, device_id_type=MESH,
        )

    def sum_copy(k, e, j):
        return pltpu.make_async_remote_copy(
            src_ref=summed.at[k, e, j], dst_ref=summed_in.at[k, e, j],
            send_sem=sum_send.at[0], recv_sem=sum_recv.at[k, j] if e == last else early_recv.at[k],
            device_id={"heads": lax.rem(x + k + 1, n_x)}, device_id_type=MESH,
        )

    def columns(j):
        return pl.ds(pl.multiple_of(j * col, col), col)

    def product(k, e, j):
        rows = heads_out[...].reshape(-1, heads_out.shape[2])
        result = jnp.dot(rows, wo_v[:, columns(j)], preferred_element_type=F32).astype(BF16)
        result = result.reshape((batch, n_c, half, col))
        for core in range(n_c):
            for n in range(batch):
                part[k, e, j, core, n] = result[n, core]
        part_copy(k, e, j).start()

    def combine(k, e, j):
        part_copy(k, e, j).wait_recv()
        both = part[k, e, j, c].astype(F32) + part_in[k, e, j].astype(F32)
        summed[k, e, j] = both.astype(BF16)
        sum_copy(k, e, j).start()

    def products(k, e):
        attend(k, e)

        def step(j, carry):
            product(k, e, j)
            return carry

        lax.fori_loop(0, n_cols, step, 0)

    def combines(k, e, lo, hi):
        def step(j, carry):
            combine(k, e, j)
            return carry

        lax.fori_loop(lo, hi, step, 0)


    up = lane // (n_lanes // 2)

    def member(i):
        g = i % groups
        return i // groups, up * (1 + g) + (1 - up) * (n_lanes - 1 - g)

    behind = min(4, n_cols)

    def blend(k, e):
        attend(k, e)

        def step(j, carry):
            @pl.when(j < n_cols)
            def _():
                product(k, e, j)

            @pl.when(j >= behind)
            def _():
                combine(k, e, j - behind)

            return carry

        lax.fori_loop(0, n_cols + behind, step, 0)

    def some_products(k, e, lo, hi):
        def step(j, carry):
            product(k, e, j)
            return carry

        lax.fori_loop(lo, hi, step, 0)

    def relays(lo, hi):
        def step(i, carry):
            relay(*member(i))
            return carry

        lax.fori_loop(lo, hi, step, 0)

    def own_relays():
        for n in range(cap):
            relay(n, 0)

    def weights_here():
        for load in loads[2:]:
            load.wait()

    soon = cap // 2 * groups
    some = n_cols // 2

    def slot_step(i, carry):
        r, d = member(i)
        tok_copy(r, d).wait_recv()
        encode([(r, d)], lambda r, d: recv_tok[r, d])

        for n in range(ahead, cap):

            @pl.when(i == (n - 1) * groups - 1)
            def _():
                send_rank(n)

        if early:

            @pl.when(i == soon - 1)
            def _():
                own_relays()

            @pl.when(i == soon)
            def _():
                relays(0, 2)

            @pl.when(i == soon + 1)
            def _():
                relays(2, groups)
                weights_here()

            @pl.when(i == soon + 2)
            def _():
                relays(groups, soon)
                project(0)

            @pl.when(i == soon + 3)
            def _():
                project(1)

            @pl.when(i == soon + 4)
            def _():
                attend(0, 0)

            @pl.when(i == soon + 5)
            def _():
                some_products(0, 0, 0, some + 2)
                combines(0, 0, 0, 2)
                some_products(0, 0, some + 2, n_cols)
                combines(0, 0, 2, 4)
                relays(soon, soon + groups)

        else:

            @pl.when(i == lag - 1)
            def _():
                own_relays()
                weights_here()

            @pl.when(i >= lag)
            def _():
                relays(i - lag, i - lag + 1)

            for n in range(cap - 1):

                @pl.when(i == (n + 1) * groups + lag - 1)
                def _():
                    project(n)

        return carry

    lax.fori_loop(0, total, slot_step, 0)
    if early:
        combines(0, 0, 4, n_cols)
        relays(soon + groups, total)
        for n in range(cap // 2, cap):
            project(n)
    else:
        relays(total - lag, total)
        project(cap - 1)
    for k in range(own):
        blend(k, last)
    for e in range(stages):
        products(own, e)

    def final_copy(j, n):
        rows = pl.ds(pl.multiple_of(n * span_len + c * half, half), half)
        return pltpu.make_async_remote_copy(
            src_ref=final_out.at[j, n], dst_ref=out_ref.at[rows, columns(j)],
            send_sem=final_send.at[0], recv_sem=final_recv.at[0],
            device_id={"rep": mate}, device_id_type=MESH,
        )

    def finish(j, carry):
        for e in range(stages):
            total = part[own, e, j, c].astype(F32) + part_in[own, e, j].astype(F32)
            for k in range(own):
                if e == last:
                    sum_copy(k, e, j).wait_recv()
                total = total + summed_in[k, e, j].astype(F32)
            final[e * batch : (e + 1) * batch] = total.astype(BF16)
        for n in range(core_spans):
            first = x * chip_spans + n
            final_out[j, n] = final[slot_sm[first + mate * core_spans]]
            final_copy(j, n).start()
            rows = pl.ds(pl.multiple_of(n * span_len + c * half, half), half)
            out_ref[rows, columns(j)] = final[slot_sm[first + c * core_spans]]
        return carry

    def arrived(ref, sem):
        pltpu.make_async_remote_copy(
            src_ref=ref, dst_ref=ref, send_sem=sem, recv_sem=sem, device_id={"rep": mate}, device_id_type=MESH
        ).wait_recv()

    for e in range(stages):
        arrived(part_in.at[own, e], own_recv.at[e])
    for k in range(own if last else 0):
        arrived(summed_in.at[k, 0], early_recv.at[k])
    lax.fori_loop(0, n_cols, finish, 0)
    sent(got_sm.at[pl.ds(0, n_lanes - 1)], idx_send.at[0])
    for r in range(cap):
        toks_sent(r)
    sent(enc.at[:, :, pl.ds(0, n_x - 1)], x_send.at[0])
    sent(enc.at[:, :, pl.ds(0, n_x)], c_send.at[0])
    sent(part_in, part_send.at[0])
    sent(summed, sum_send.at[0])
    sent(final_out, final_send.at[0])
    pltpu.make_async_remote_copy(
        src_ref=final_out, dst_ref=final_out, send_sem=final_send.at[0], recv_sem=final_recv.at[0],
        device_id={"rep": mate}, device_id_type=MESH,
    ).wait_recv()


def shards(queries, span_states, store, entry_ids, owners, w_key, w_value, w_out):
    n_lanes, n_x, n_c = (lax.axis_size(name) for name in ("lanes", "heads", "rep"))
    spans, fanout = entry_ids.shape
    requests = spans * fanout
    cap = max(2, (requests + n_lanes - 1) // n_lanes)
    span_len = queries.shape[0] // spans
    tok_dev, width = store.shape[1:]
    tokens = tok_dev * n_x * n_c
    head_cols, model = w_out.shape
    out_rows = queries.shape[0] // (n_x * n_c)
    n_cols = 8
    core_spans = spans // (n_x * n_c)
    chip_spans = spans // n_x
    stages = 2 if early_spans(n_x, n_lanes, cap, spans, fanout) else 1
    batch = chip_spans // stages
    half = span_len // n_c
    col = model // n_cols
    lanes_wide = -(-(n_lanes * cap) // 128) * 128
    dma = pltpu.SemaphoreType.DMA
    hbm = pl.BlockSpec(memory_space=pl.ANY)
    smem = pl.BlockSpec(memory_space=pltpu.SMEM)
    return pl.pallas_call(
        functools.partial(fused, n_lanes, n_x, n_c, cap, n_cols),
        out_shape=pltpu.VMEM((out_rows, model), BF16),
        in_specs=[smem, smem] + [hbm] * 6,
        out_specs=pl.BlockSpec(memory_space=pltpu.VMEM),
        scratch_shapes=[
            pltpu.VMEM((spans, span_len, head_cols), BF16),
            pltpu.VMEM((spans, span_len, width), BF16),
            pltpu.VMEM(store.shape, BF16),
            pltpu.VMEM(w_key.shape, BF16),
            pltpu.VMEM(w_value.shape, BF16),
            pltpu.VMEM(w_out.shape, BF16),
            pltpu.VMEM((8, lanes_wide), jnp.int32),
            pltpu.VMEM((8, lanes_wide), jnp.int32),
            pltpu.SMEM((8, lanes_wide), jnp.int32),
            pltpu.SMEM((8, lanes_wide), jnp.int32),
            pltpu.SMEM((n_lanes, 8, lanes_wide), jnp.int32),
            pltpu.SMEM((requests,), jnp.int32),
            pltpu.SMEM((spans,), jnp.int32),
            pltpu.SMEM((spans,), jnp.int32),
            pltpu.VMEM((cap, n_lanes, tok_dev, width), BF16),
            pltpu.VMEM((cap, n_lanes, tok_dev, width), BF16),
            pltpu.VMEM((cap, n_lanes, n_x * n_c, tok_dev, width), BF16),
            pltpu.VMEM((cap, n_lanes, tokens, head_cols), BF16),
            pltpu.VMEM((cap, n_lanes, tokens, head_cols), BF16),
            pltpu.VMEM((batch, span_len, head_cols), BF16),
            pltpu.VMEM((n_x, stages, n_cols, n_c, batch, half, col), BF16),
            pltpu.VMEM((n_x, stages, n_cols, batch, half, col), BF16),
            pltpu.VMEM((n_x - 1, stages, n_cols, batch, half, col), BF16),
            pltpu.VMEM((n_x - 1, stages, n_cols, batch, half, col), BF16),
            pltpu.VMEM((chip_spans, half, col), BF16),
            pltpu.VMEM((n_cols, core_spans, half, col), BF16),
            dma((6,)),
            dma((2,)),
            dma((1,)),
            dma((n_lanes - 1,)),
            dma((cap,)),
            dma((cap, n_lanes - 1)),
            dma((1,)),
            dma((1,)),
            dma((cap, n_lanes, n_x - 1)),
            dma((cap,)),
            dma((1,)),
            dma((n_x - 1, stages, n_cols)),
            dma((stages,)),
            dma((1,)),
            dma((n_x - 1, n_cols)),
            dma((n_x - 1,)),
            dma((1,)),
            dma((1,)),
        ],
        compiler_params=pltpu.CompilerParams(
            collective_id=0, has_side_effects=True, vmem_limit_bytes=60000000
        ),
    )(
        owners.T,
        entry_ids.T,
        queries.reshape(spans, span_len, head_cols),
        span_states.reshape(spans, span_len, width),
        store,
        w_key,
        w_value,
        w_out,
    )


def solution(mesh):
    return jax.shard_map(
        shards,
        mesh=mesh,
        in_specs=(
            P(("groups", "lanes"), ("heads", "rep")),
            P(("groups", "lanes"), None),
            P(("groups", "lanes"), ("heads", "rep"), None),
            P(("groups", "lanes"), None),
            P(("groups", "lanes"), None),
            P(None, ("heads", "rep")),
            P(None, ("heads", "rep")),
            P(("heads", "rep"), None),
        ),
        out_specs=P(("groups", "lanes", "heads", "rep"), None),
        check_vma=False,
    )
```

```python
import functools
import itertools

import jax
import jax.numpy as jnp
from jax import lax
from jax.experimental import pallas as pl
from jax.experimental.pallas import tpu as pltpu
from jax.sharding import PartitionSpec as P

HD = 128
ENCODER_HEAD_DIM = 128
MESH = pl.DeviceIdType.MESH
F32 = jnp.float32
BF16 = jnp.bfloat16


def softmax_parts(parts):
    top = functools.reduce(jnp.maximum, [jnp.max(p, axis=-1, keepdims=True) for p in parts])
    exps = [jnp.exp(p - top) for p in parts]
    total = functools.reduce(jnp.add, [jnp.sum(e, axis=-1, keepdims=True) for e in exps])
    inv = 1.0 / total
    return [(e * inv).astype(BF16) for e in exps]


def dot_t(a, b):
    return lax.dot_general(a, b, (((1,), (1,)), ((), ())), preferred_element_type=F32)


def early_spans(n_x, n_lanes, cap, spans, fanout):
    whole = n_x == 2 and cap == n_lanes == 4 and fanout == 2 and spans == 2 * n_lanes
    return spans // n_x // 2 if whole else 0


def fused(
    n_lanes, n_x, n_c, cap, n_cols,
    owner_ref, entry_ref, query_hbm, states_hbm, store_hbm, wk_hbm, wv_hbm, wo_hbm,
    out_ref,
    query_v, states_v, store_v, wk_v, wv_v, wo_v,
    table, span_table, span_sm, own_sm, got_sm, rank_sm, virtual_sm, slot_sm,
    send_tok, recv_tok, enc, keys, values, heads_out,
    part, part_in, summed, summed_in, final, final_out,
    load_sem, local_sem, idx_send, idx_recv, tok_sends, tok_recvs, x_send, c_send, x_recvs, c_recvs,
    part_send, part_recv, own_recv, sum_send, sum_recv, early_recv, final_send, final_recv,
):
    lane = lax.axis_index("lanes")
    x = lax.axis_index("heads")
    c = lax.axis_index("rep")
    mate = n_c - 1 - c
    fanout, spans = owner_ref.shape
    requests = spans * fanout
    width = store_v.shape[2]
    span_len = query_v.shape[1]
    chip_spans = spans // n_x
    core_spans = chip_spans // n_c
    col = wo_v.shape[1] // n_cols
    half = span_len // n_c
    quarter = x * n_c + c
    early = early_spans(n_x, n_lanes, cap, spans, fanout)
    stages = part.shape[1]
    own = n_x - 1
    last = stages - 1
    batch = chip_spans // stages

    loads = [
        pltpu.make_async_copy(src, dst, load_sem.at[i])
        for i, (src, dst) in enumerate(
            (
                (store_hbm, store_v),
                (states_hbm, states_v),
                (wk_hbm, wk_v),
                (wv_hbm, wv_v),
                (query_hbm, query_v),
                (wo_hbm, wo_v),
            )
        )
    ]
    for load in loads[:2]:
        load.start()

    barrier = pltpu.get_barrier_semaphore()
    for d in range(1, n_lanes):
        pl.semaphore_signal(barrier, inc=1, device_id={"lanes": lax.rem(lane + d, n_lanes)}, device_id_type=MESH)
    for d in range(1, n_x):
        pl.semaphore_signal(barrier, inc=1, device_id={"heads": lax.rem(x + d, n_x)}, device_id_type=MESH)
    pl.semaphore_signal(barrier, inc=1, device_id={"rep": mate}, device_id_type=MESH)

    owner = [owner_ref[j % fanout, j // fanout] for j in range(requests)]
    ranks = []
    if early:
        word = [
            sum(jnp.where(owner[s * fanout + f] == o, 1 << (4 * o), 0) for f in range(fanout) for o in range(n_lanes))
            for s in range(spans)
        ]
        target = sum((cap // 2) << (4 * o) for o in range(n_lanes))
        chosen = list(itertools.combinations(range(chip_spans), early))
        sums = [[sum(word[h * chip_spans + s] for s in some) for some in chosen] for h in range(n_x)]
        mask = jnp.int32(0)
        for a, some in enumerate(chosen):
            for b, others in enumerate(chosen):
                bits = sum(1 << s for s in some) + sum(1 << (chip_spans + s) for s in others)
                mask = jnp.where(sums[0][a] + sums[1][b] == target, bits, mask)
        first, later = jnp.int32(0), jnp.int32(target)
        slot = []
        for s in range(spans):
            if s % chip_spans == 0:
                n_first, n_later = jnp.int32(0), jnp.int32(early)
            taken = ((mask >> s) & 1) == 1
            ahead = jnp.where(taken, first, later)
            for f in range(fanout):
                ranks.append(
                    sum(jnp.where(owner[s * fanout + f] == o, (ahead >> (4 * o)) & 15, 0) for o in range(n_lanes))
                )
            first, later = first + jnp.where(taken, word[s], 0), later + jnp.where(taken, 0, word[s])
            slot.append(jnp.where(taken, n_first, n_later))
            n_first, n_later = n_first + jnp.where(taken, 1, 0), n_later + jnp.where(taken, 0, 1)
        for s in range(spans):
            base = s // chip_spans * chip_spans
            slot_sm[s] = jnp.minimum(slot[s], chip_spans - 1)
            virtual_sm[s] = sum(jnp.where(slot[base + i] == s - base, base + i, 0) for i in range(chip_spans))
    else:
        for j in range(requests):
            ranks.append(sum((owner[i] == owner[j]).astype(jnp.int32) for i in range(j)) + jnp.int32(0))
        for s in range(spans):
            slot_sm[s] = s % chip_spans
            virtual_sm[s] = s
    place = lax.broadcasted_iota(jnp.int32, table.shape, 1)
    entries = jnp.zeros(table.shape, jnp.int32)
    whose = jnp.zeros(table.shape, jnp.int32)
    for j, rank in enumerate(ranks):
        rank_sm[j] = jnp.minimum(rank, cap - 1)
        hit = place == owner[j] * cap + rank
        entries = jnp.where(hit, entry_ref[j % fanout, j // fanout], entries)
        whose = jnp.where(hit, j // fanout, whose)
    table[...] = entries
    span_table[...] = whose
    pl.semaphore_wait(barrier, n_lanes + n_x - 1)

    def idx_copy(d):
        return pltpu.make_async_remote_copy(
            src_ref=table, dst_ref=got_sm.at[lane], send_sem=idx_send.at[0], recv_sem=idx_recv.at[d - 1],
            device_id={"lanes": lax.rem(lane + d, n_lanes)}, device_id_type=MESH,
        )

    for d in range(1, n_lanes):
        idx_copy(d).start()
    to_sm = pltpu.make_async_copy(span_table, span_sm, local_sem.at[0])
    to_sm.start()
    own_to_sm = pltpu.make_async_copy(table, own_sm, local_sem.at[1])
    own_to_sm.start()
    to_sm.wait()
    own_to_sm.wait()
    loads[0].wait()
    loads[1].wait()
    for load in loads[2:]:
        load.start()

    def tok_copy(r, d):
        return pltpu.make_async_remote_copy(
            src_ref=send_tok.at[r, d], dst_ref=recv_tok.at[r, d],
            send_sem=tok_sends.at[r], recv_sem=tok_recvs.at[r, d - 1],
            device_id={"lanes": lax.rem(lane + d, n_lanes)}, device_id_type=MESH,
        )

    def sent(ref, sem):
        pltpu.make_async_remote_copy(
            src_ref=ref, dst_ref=ref, send_sem=sem, recv_sem=sem, device_id={"rep": mate}, device_id_type=MESH
        ).wait_send()

    def toks_sent(r):
        sent(send_tok.at[r, pl.ds(1, n_lanes - 1)], tok_sends.at[r])

    def send_one(r, d):
        who = lax.rem(lane + d, n_lanes)
        send_tok[r, d] = store_v[got_sm[who, 0, lane * cap + r]]
        tok_copy(r, d).start()

    def send_rank(r):
        def one(d, carry):
            send_one(r, d)
            return carry

        lax.fori_loop(1, n_lanes, one, 0)

    def x_copy(r, s, d):
        return pltpu.make_async_remote_copy(
            src_ref=enc.at[r, s, quarter], dst_ref=enc.at[r, s, quarter],
            send_sem=x_send.at[0], recv_sem=x_recvs.at[r, s, d - 1],
            device_id={"heads": lax.rem(x + d, n_x)}, device_id_type=MESH,
        )

    def c_copy(r, s, block):
        return pltpu.make_async_remote_copy(
            src_ref=enc.at[r, s, block], dst_ref=enc.at[r, s, block],
            send_sem=c_send.at[0], recv_sem=c_recvs.at[r],
            device_id={"rep": mate}, device_id_type=MESH,
        )

    def source(d):
        return lax.rem(lane - d + n_lanes, n_lanes)

    def encode(group, fetch):
        tokens = [fetch(r, d) for r, d in group]
        states = [states_v[span_sm[0, source(d) * cap + r]] for r, d in group]
        heads = [
            (n, slice(h * ENCODER_HEAD_DIM, (h + 1) * ENCODER_HEAD_DIM))
            for n in range(len(group))
            for h in range(width // ENCODER_HEAD_DIM)
        ]
        logits = [dot_t(tokens[n][:, cols], states[n][:, cols]) * ENCODER_HEAD_DIM ** (-0.5) for n, cols in heads]
        weights = [softmax_parts([logit])[0] for logit in logits]
        mixed = [
            jnp.dot(weight, states[n][:, cols], preferred_element_type=F32) for weight, (n, cols) in zip(weights, heads)
        ]
        for mix, (n, cols) in zip(mixed, heads):
            r, d = group[n]
            enc[r, source(d), quarter, :, cols] = (tokens[n][:, cols].astype(F32) + mix).astype(BF16)
        for r, d in group:
            s = source(d)
            for k in range(1, n_x):
                x_copy(r, s, k).start()
            c_copy(r, s, quarter).start()

    def relay(r, d):
        s = source(d)
        for k in range(1, n_x):
            block = lax.rem(x - k + n_x, n_x) * n_c + c
            pltpu.make_async_remote_copy(
                src_ref=enc.at[r, s, block], dst_ref=enc.at[r, s, block],
                send_sem=x_send.at[0], recv_sem=x_recvs.at[r, s, k - 1],
                device_id={"rep": mate}, device_id_type=MESH,
            ).wait_recv()
            c_copy(r, s, block).start()

    encode([(r, 0) for r in range(cap)], lambda r, d: store_v[own_sm[0, lane * cap + r]])
    ahead = min(2, cap)
    for d in sorted(range(1, n_lanes), key=lambda d: min(d, n_lanes - d)):
        idx_copy(d).wait_recv()
        send_one(0, n_lanes - d)
    for r in range(1, ahead):

        @pl.when(c == 0)
        def _():
            send_rank(r)

    groups = n_lanes - 1
    total = cap * groups
    lag = min(3, groups)
    lane_chunk = min(n_lanes, 4)

    def settle(r):
        ref = enc.at[r, :, pl.ds(0, n_x)]
        pltpu.make_async_remote_copy(
            src_ref=ref, dst_ref=ref, send_sem=c_send.at[0], recv_sem=c_recvs.at[r],
            device_id={"rep": mate}, device_id_type=MESH,
        ).wait_recv()

    def project(r):
        settle(r)

        def chunk(g, carry):
            some = pl.ds(g * lane_chunk, lane_chunk)
            rows = enc[r, some].reshape(-1, width)
            for weight, target in ((wk_v, keys), (wv_v, values)):
                result = jnp.dot(rows, weight[...], preferred_element_type=F32).astype(BF16)
                target[r, some] = result.reshape((lane_chunk,) + target.shape[2:])
            return carry

        lax.fori_loop(0, n_lanes // lane_chunk, chunk, 0)

    def attend(k, e):
        first = lax.rem(x + k + 1, n_x) * chip_spans + e * batch
        which = [virtual_sm[first + n] for n in range(batch)]
        slots = [[(rank_sm[s * fanout + f], owner_ref[f, s]) for f in range(fanout)] for s in which]
        heads = [(n, slice(h * HD, (h + 1) * HD)) for n in range(batch) for h in range(query_v.shape[2] // HD)]
        logits = [
            [dot_t(query_v[which[n], :, cols], keys[r, o, :, cols]) * HD ** (-0.5) for r, o in slots[n]]
            for n, cols in heads
        ]
        weights = [softmax_parts(parts) for parts in logits]
        mixed = [
            functools.reduce(
                jnp.add,
                [
                    jnp.dot(w, values[r, o, :, cols], preferred_element_type=F32)
                    for w, (r, o) in zip(parts, slots[n])
                ],
            )
            for parts, (n, cols) in zip(weights, heads)
        ]
        for mix, (n, cols) in zip(mixed, heads):
            heads_out[n, :, cols] = mix.astype(BF16)

    def part_copy(k, e, j):
        return pltpu.make_async_remote_copy(
            src_ref=part.at[k, e, j, mate], dst_ref=part_in.at[k, e, j],
            send_sem=part_send.at[0], recv_sem=part_recv.at[k, e, j] if k < own else own_recv.at[e],
            device_id={"rep": mate}, device_id_type=MESH,
        )

    def sum_copy(k, e, j):
        return pltpu.make_async_remote_copy(
            src_ref=summed.at[k, e, j], dst_ref=summed_in.at[k, e, j],
            send_sem=sum_send.at[0], recv_sem=sum_recv.at[k, j] if e == last else early_recv.at[k],
            device_id={"heads": lax.rem(x + k + 1, n_x)}, device_id_type=MESH,
        )

    def columns(j):
        return pl.ds(pl.multiple_of(j * col, col), col)

    def product(k, e, j):
        rows = heads_out[...].reshape(-1, heads_out.shape[2])
        result = jnp.dot(rows, wo_v[:, columns(j)], preferred_element_type=F32).astype(BF16)
        result = result.reshape((batch, n_c, half, col))
        for core in range(n_c):
            for n in range(batch):
                part[k, e, j, core, n] = result[n, core]
        part_copy(k, e, j).start()

    def combine(k, e, j):
        part_copy(k, e, j).wait_recv()
        both = part[k, e, j, c].astype(F32) + part_in[k, e, j].astype(F32)
        summed[k, e, j] = both.astype(BF16)
        sum_copy(k, e, j).start()

    def products(k, e):
        attend(k, e)

        def step(j, carry):
            product(k, e, j)
            return carry

        lax.fori_loop(0, n_cols, step, 0)

    def combines(k, e, lo, hi):
        def step(j, carry):
            combine(k, e, j)
            return carry

        lax.fori_loop(lo, hi, step, 0)


    up = lane // (n_lanes // 2)

    def member(i):
        g = i % groups
        return i // groups, up * (1 + g) + (1 - up) * (n_lanes - 1 - g)

    behind = min(4, n_cols)

    def blend(k, e):
        attend(k, e)

        def step(j, carry):
            @pl.when(j < n_cols)
            def _():
                product(k, e, j)

            @pl.when(j >= behind)
            def _():
                combine(k, e, j - behind)

            return carry

        lax.fori_loop(0, n_cols + behind, step, 0)

    def some_products(k, e, lo, hi):
        def step(j, carry):
            product(k, e, j)
            return carry

        lax.fori_loop(lo, hi, step, 0)

    def relays(lo, hi):
        def step(i, carry):
            relay(*member(i))
            return carry

        lax.fori_loop(lo, hi, step, 0)

    def own_relays():
        for n in range(cap):
            relay(n, 0)

    def weights_here():
        for load in loads[2:]:
            load.wait()

    soon = cap // 2 * groups
    some = n_cols // 2

    def slot_step(i, carry):
        r, d = member(i)
        tok_copy(r, d).wait_recv()
        encode([(r, d)], lambda r, d: recv_tok[r, d])

        for n in range(1, ahead):

            @pl.when(jnp.logical_and(i == 0, c > 0))
            def _():
                send_rank(n)

        for n in range(ahead, cap):

            @pl.when(i == (n - 1) * groups - 1)
            def _():
                send_rank(n)

        if early:

            @pl.when(i == soon - 1)
            def _():
                own_relays()

            @pl.when(i == soon)
            def _():
                relays(0, 2)

            @pl.when(i == soon + 1)
            def _():
                relays(2, groups)
                weights_here()

            @pl.when(i == soon + 2)
            def _():
                relays(groups, soon)
                project(0)

            @pl.when(i == soon + 3)
            def _():
                project(1)

            @pl.when(i == soon + 4)
            def _():
                attend(0, 0)

            @pl.when(i == soon + 5)
            def _():
                some_products(0, 0, 0, some + 2)
                combines(0, 0, 0, 2)
                some_products(0, 0, some + 2, n_cols)
                combines(0, 0, 2, 4)
                relays(soon, soon + groups)

        else:

            @pl.when(i == lag - 1)
            def _():
                own_relays()
                weights_here()

            @pl.when(i >= lag)
            def _():
                relays(i - lag, i - lag + 1)

            for n in range(cap - 1):

                @pl.when(i == (n + 1) * groups + lag - 1)
                def _():
                    project(n)

        return carry

    lax.fori_loop(0, total, slot_step, 0)
    if early:
        combines(0, 0, 4, n_cols)
        relays(soon + groups, total)
        for n in range(cap // 2, cap):
            project(n)
    else:
        relays(total - lag, total)
        project(cap - 1)
    for k in range(own):
        blend(k, last)
    for e in range(stages):
        products(own, e)

    def final_copy(j, n):
        rows = pl.ds(pl.multiple_of(n * span_len + c * half, half), half)
        return pltpu.make_async_remote_copy(
            src_ref=final_out.at[j, n], dst_ref=out_ref.at[rows, columns(j)],
            send_sem=final_send.at[0], recv_sem=final_recv.at[0],
            device_id={"rep": mate}, device_id_type=MESH,
        )

    def finish(j, carry):
        for e in range(stages):
            total = part[own, e, j, c].astype(F32) + part_in[own, e, j].astype(F32)
            for k in range(own):
                if e == last:
                    sum_copy(k, e, j).wait_recv()
                total = total + summed_in[k, e, j].astype(F32)
            final[e * batch : (e + 1) * batch] = total.astype(BF16)
        for n in range(core_spans):
            first = x * chip_spans + n
            final_out[j, n] = final[slot_sm[first + mate * core_spans]]
            final_copy(j, n).start()
            rows = pl.ds(pl.multiple_of(n * span_len + c * half, half), half)
            out_ref[rows, columns(j)] = final[slot_sm[first + c * core_spans]]
        return carry

    def arrived(ref, sem):
        pltpu.make_async_remote_copy(
            src_ref=ref, dst_ref=ref, send_sem=sem, recv_sem=sem, device_id={"rep": mate}, device_id_type=MESH
        ).wait_recv()

    for e in range(stages):
        arrived(part_in.at[own, e], own_recv.at[e])
    for k in range(own if last else 0):
        arrived(summed_in.at[k, 0], early_recv.at[k])
    lax.fori_loop(0, n_cols, finish, 0)
    sent(got_sm.at[pl.ds(0, n_lanes - 1)], idx_send.at[0])
    for r in range(cap):
        toks_sent(r)
    sent(enc.at[:, :, pl.ds(0, n_x - 1)], x_send.at[0])
    sent(enc.at[:, :, pl.ds(0, n_x)], c_send.at[0])
    sent(part_in, part_send.at[0])
    sent(summed, sum_send.at[0])
    sent(final_out, final_send.at[0])
    pltpu.make_async_remote_copy(
        src_ref=final_out, dst_ref=final_out, send_sem=final_send.at[0], recv_sem=final_recv.at[0],
        device_id={"rep": mate}, device_id_type=MESH,
    ).wait_recv()


def shards(queries, span_states, store, entry_ids, owners, w_key, w_value, w_out):
    n_lanes, n_x, n_c = (lax.axis_size(name) for name in ("lanes", "heads", "rep"))
    spans, fanout = entry_ids.shape
    requests = spans * fanout
    cap = max(2, (requests + n_lanes - 1) // n_lanes)
    span_len = queries.shape[0] // spans
    tok_dev, width = store.shape[1:]
    tokens = tok_dev * n_x * n_c
    head_cols, model = w_out.shape
    out_rows = queries.shape[0] // (n_x * n_c)
    n_cols = 8
    core_spans = spans // (n_x * n_c)
    chip_spans = spans // n_x
    stages = 2 if early_spans(n_x, n_lanes, cap, spans, fanout) else 1
    batch = chip_spans // stages
    half = span_len // n_c
    col = model // n_cols
    lanes_wide = -(-(n_lanes * cap) // 128) * 128
    dma = pltpu.SemaphoreType.DMA
    hbm = pl.BlockSpec(memory_space=pl.ANY)
    smem = pl.BlockSpec(memory_space=pltpu.SMEM)
    return pl.pallas_call(
        functools.partial(fused, n_lanes, n_x, n_c, cap, n_cols),
        out_shape=pltpu.VMEM((out_rows, model), BF16),
        in_specs=[smem, smem] + [hbm] * 6,
        out_specs=pl.BlockSpec(memory_space=pltpu.VMEM),
        scratch_shapes=[
            pltpu.VMEM((spans, span_len, head_cols), BF16),
            pltpu.VMEM((spans, span_len, width), BF16),
            pltpu.VMEM(store.shape, BF16),
            pltpu.VMEM(w_key.shape, BF16),
            pltpu.VMEM(w_value.shape, BF16),
            pltpu.VMEM(w_out.shape, BF16),
            pltpu.VMEM((8, lanes_wide), jnp.int32),
            pltpu.VMEM((8, lanes_wide), jnp.int32),
            pltpu.SMEM((8, lanes_wide), jnp.int32),
            pltpu.SMEM((8, lanes_wide), jnp.int32),
            pltpu.SMEM((n_lanes, 8, lanes_wide), jnp.int32),
            pltpu.SMEM((requests,), jnp.int32),
            pltpu.SMEM((spans,), jnp.int32),
            pltpu.SMEM((spans,), jnp.int32),
            pltpu.VMEM((cap, n_lanes, tok_dev, width), BF16),
            pltpu.VMEM((cap, n_lanes, tok_dev, width), BF16),
            pltpu.VMEM((cap, n_lanes, n_x * n_c, tok_dev, width), BF16),
            pltpu.VMEM((cap, n_lanes, tokens, head_cols), BF16),
            pltpu.VMEM((cap, n_lanes, tokens, head_cols), BF16),
            pltpu.VMEM((batch, span_len, head_cols), BF16),
            pltpu.VMEM((n_x, stages, n_cols, n_c, batch, half, col), BF16),
            pltpu.VMEM((n_x, stages, n_cols, batch, half, col), BF16),
            pltpu.VMEM((n_x - 1, stages, n_cols, batch, half, col), BF16),
            pltpu.VMEM((n_x - 1, stages, n_cols, batch, half, col), BF16),
            pltpu.VMEM((chip_spans, half, col), BF16),
            pltpu.VMEM((n_cols, core_spans, half, col), BF16),
            dma((6,)),
            dma((2,)),
            dma((1,)),
            dma((n_lanes - 1,)),
            dma((cap,)),
            dma((cap, n_lanes - 1)),
            dma((1,)),
            dma((1,)),
            dma((cap, n_lanes, n_x - 1)),
            dma((cap,)),
            dma((1,)),
            dma((n_x - 1, stages, n_cols)),
            dma((stages,)),
            dma((1,)),
            dma((n_x - 1, n_cols)),
            dma((n_x - 1,)),
            dma((1,)),
            dma((1,)),
        ],
        compiler_params=pltpu.CompilerParams(
            collective_id=0, has_side_effects=True, vmem_limit_bytes=60000000
        ),
    )(
        owners.T,
        entry_ids.T,
        queries.reshape(spans, span_len, head_cols),
        span_states.reshape(spans, span_len, width),
        store,
        w_key,
        w_value,
        w_out,
    )


def solution(mesh):
    return jax.shard_map(
        shards,
        mesh=mesh,
        in_specs=(
            P(("groups", "lanes"), ("heads", "rep")),
            P(("groups", "lanes"), None),
            P(("groups", "lanes"), ("heads", "rep"), None),
            P(("groups", "lanes"), None),
            P(("groups", "lanes"), None),
            P(None, ("heads", "rep")),
            P(None, ("heads", "rep")),
            P(("heads", "rep"), None),
        ),
        out_specs=P(("groups", "lanes", "heads", "rep"), None),
        check_vma=False,
    )
```
